512 devices in a mesh: row: 32 (over z, core), col: 16 (over x, y).
Axes of the slice: x: 4, y: 4, z: 16, core: 2. Of those that a mesh axis runs over, the one named last changes fastest.
Arguments:
- front_entries: float32 [16384, 16384], P('row', 'col'), may hold values from 0 to 3, as said below
- tile_group: int32 [32], replicated, may hold values from 0 to 3
- child_factor: bfloat16 [16384, 256], P('row', 'col'), may hold values from -0.375 to 0.375
- row_map: int32 [128], replicated, may hold values from 0 to 127, as said below
Outputs:
- factor_panels: bfloat16 [16384, 512], P('row', 'col')
- schur_block: float32 [16384, 16384], P('row', 'col')
The draws below stay inside these ranges and needn't reach their ends.
Inputs may be any that keep to these rules, and one draw needn't show every extreme that they name: `front_entries`: Symmetric; assembled is positive definite. `row_map`: A permutation of the parent tiles. The tile in row block r (blocks of 512 rows) goes to a parent tile in row block r or in the row block whose index differs from r in the highest bit.
All inputs are finite; a program needn't handle non-finite values.
Results may differ from the reference program's by a relative error of at most 0.0026.
Values may be sent and summed in bfloat16 or wider, within the bound.
A program may use at most 64 MiB of HBM per device.

```python
import jax
import jax.numpy as jnp
from jax import lax

F = 16384
PW = 256
NP = 2
KC = 256
TS = 128
MT = 512
N_ROW = 32
N_COL = 16


def draw_front_entries(key, part):
    point_key = jax.random.fold_in(key, 11)
    shift_key = jax.random.fold_in(key, 23)
    points = jax.random.uniform(point_key, (F, 3), jnp.float32)
    diag_shift = jnp.exp(jax.random.uniform(shift_key, (F,), jnp.float32, jnp.log(0.5), jnp.log(2.0)))
    length_scale = 2.0 * float(F) ** (-1.0 / 3.0)
    distance_sq = jnp.zeros((F, F), jnp.float32)
    for dim_index in range(3):
        offset_dim = points[:, dim_index][:, None] - points[:, dim_index][None, :]
        distance_sq = distance_sq + offset_dim * offset_dim
    kernel = jnp.exp(-jnp.sqrt(distance_sq) / length_scale)
    diag_ids = jnp.arange(F)
    return kernel.at[diag_ids, diag_ids].add(diag_shift)


def draw_row_map(key, part):
    tile_count = F // TS // N_ROW
    half_rows = N_ROW // 2
    pair_keys = jax.random.split(jax.random.fold_in(key, 37), half_rows)
    shuffles = jax.vmap(lambda single: jax.random.permutation(single, 2 * tile_count))(pair_keys)
    device = jnp.arange(half_rows, dtype=jnp.int32)[:, None]
    target = (device + shuffles // tile_count * half_rows) * tile_count + shuffles % tile_count
    child_first = target[:, :tile_count].reshape(-1)
    child_second = target[:, tile_count:].reshape(-1)
    return jnp.concatenate([child_first, child_second]).astype(jnp.int32)


def with_ends(drawn, stream_key, smallest, high):
    dims = drawn.shape
    index_at = [jax.random.randint(jax.random.fold_in(stream_key, axis), (), 0, dims[axis]) for axis in range(len(dims))]
    drawn = drawn.at[tuple(index_at)].set(smallest)
    longest = dims.index(max(dims))
    index_at[longest] = (index_at[longest] + 1) % dims[longest]
    return drawn.at[tuple(index_at)].set(high)


def levels(key, shape, cuts, smallest, largest):
    gain, own = 1.0, jax.random.fold_in(key, 6)
    for dim, blocks in cuts:
        heights = jnp.exp(jax.random.uniform(jax.random.fold_in(own, dim), (blocks,), jnp.float32, smallest / len(cuts), largest / len(cuts)))
        gain = gain * jnp.repeat(heights, shape[dim] // blocks).reshape([-1 if axis == dim else 1 for axis in range(len(shape))])
    return gain


def bell_draw(rng, dims, deviation, reach, shards=(), held_as=jnp.bfloat16):
    level = levels(rng, dims, shards, -0.22, 0.18) if shards else 1.0
    values = jax.random.normal(rng, dims, jnp.float32) * deviation * level
    return jnp.minimum(jnp.maximum(values, -reach), reach).astype(held_as)


def setup_inputs(seed: int = 0) -> dict:
    streams_of = jax.random.split(jax.random.key(seed), 5)
    return {
        "front_entries": draw_front_entries(jax.random.fold_in(streams_of[4], 71), 0),
        "tile_group": with_ends(jax.random.randint(streams_of[1], (F // MT,), 0, 4), jax.random.fold_in(streams_of[1], 1), 0, 3).astype(jnp.int32),
        "child_factor": bell_draw(streams_of[2], (F, KC), KC ** -0.5, 0.375, ((0, 32), (1, 16))),
        "row_map": draw_row_map(jax.random.fold_in(streams_of[4], 71), 0),
    }


def reference(front_entries, tile_group, child_factor, row_map):
    block_rows = F // N_ROW
    row_share = PW // N_ROW
    col_share = PW // N_COL
    mask_tiles = F // MT
    same_group = (tile_group[:, None] == tile_group[None, :]).astype(jnp.float32)
    masked = (front_entries.reshape(mask_tiles, MT, mask_tiles, MT) * same_group[:, None, :, None]).reshape(F, F)
    child_tiles = F // TS
    half_tiles = child_tiles // 2
    pieces = child_factor.reshape(child_tiles, TS, KC)
    child_first = jnp.zeros((child_tiles, TS, KC), jnp.bfloat16).at[row_map[:half_tiles]].set(pieces[:half_tiles])
    child_second = jnp.zeros((child_tiles, TS, KC), jnp.bfloat16).at[row_map[half_tiles:]].set(pieces[half_tiles:])
    child_wide = jnp.concatenate([child_first.reshape(F, KC), child_second.reshape(F, KC)], axis=1).astype(jnp.float32)
    assembled = masked + jnp.dot(child_wide, child_wide.T, precision=lax.Precision.HIGHEST)
    block_ids = jnp.arange(N_ROW, dtype=jnp.int32)
    pivots = (block_ids[None, :, None] * block_rows + jnp.arange(NP, dtype=jnp.int32)[:, None, None] * row_share + jnp.arange(row_share, dtype=jnp.int32)[None, None, :]).reshape(-1)
    pivot_done = NP * row_share
    remaining = (block_ids[:, None] * block_rows + pivot_done + jnp.arange(block_rows - pivot_done, dtype=jnp.int32)[None, :]).reshape(-1)
    pivot_order = jnp.concatenate([pivots, remaining]).astype(jnp.int32)
    inverse = jnp.zeros((F,), jnp.int32).at[pivot_order].set(jnp.arange(F, dtype=jnp.int32))
    working = assembled[pivot_order][:, pivot_order]
    columns = []
    for k in range(NP):
        low = k * PW
        high = low + PW
        lower_factor = jnp.linalg.cholesky(working[low:high, low:high])
        below = lax.linalg.triangular_solve(lower_factor, working[high:, low:high], left_side=False, lower=True, transpose_a=True)
        panel = jnp.concatenate([jnp.zeros((low, PW), jnp.float32), lower_factor, below], axis=0).astype(jnp.bfloat16)
        columns.append(panel)
        lead_rows = panel[high:].astype(jnp.float32)
        working = working.at[high:, high:].add(-jnp.dot(lead_rows, lead_rows.T, precision=lax.Precision.HIGHEST))
    factor_full = jnp.concatenate(columns, axis=1)
    factor_store = factor_full[inverse]
    factor_panels = factor_store.reshape(F, NP, N_COL, col_share).transpose(0, 2, 1, 3).reshape(F, NP * PW)
    pivot_total = NP * PW
    trailing = jnp.zeros((F, F), jnp.float32).at[pivot_total:, pivot_total:].set(working[pivot_total:, pivot_total:])
    schur_block = trailing[inverse][:, inverse]
    return (factor_panels, schur_block)
```

```python
import functools

import jax
import jax.numpy as jnp
from jax import lax
from jax.experimental import pallas as pl
from jax.experimental.pallas import tpu as pltpu
from jax.sharding import PartitionSpec as P

PW = 256
NP = 2
TS = 128
MT = 512
NB = 32
SUB = 8
F32 = jnp.float32
BF16 = jnp.bfloat16
MESH = pl.DeviceIdType.MESH


def loop(count, body):
    def step(i, carry):
        body(i)
        return carry

    lax.fori_loop(0, count, step, 0)


def comm_kernel(
    zin, srow, scol, child, pick,
    diag, vpiv, strip_r, strip_c, v_r, v_c,
    zbuf, partner, placed, dpiece, vpiece,
    z_s, z_r, p_s, p_r, t_s, t_r,
    plane_s, plane_r, ring_s, ring_r, sib_s, sib_r,
):
    r = lax.axis_index("row")
    c = lax.axis_index("col")
    rows = lax.axis_size("row")
    cols = lax.axis_size("col")
    z = r // 2
    core = r % 2
    chips = rows // 2
    t_row = 2 * c + core
    t_col = z
    t_self = jnp.logical_and(t_row == r, t_col == c)

    barrier = pltpu.get_barrier_semaphore()

    def hello_row(i):
        pl.semaphore_signal(barrier, inc=1, device_id=(lax.rem(r + i + 1, rows), c), device_id_type=MESH)

    def hello_col(i):
        pl.semaphore_signal(barrier, inc=1, device_id=(r, lax.rem(c + i + 1, cols)), device_id_type=MESH)

    loop(rows - 1, hello_row)
    loop(cols - 1, hello_col)

    @pl.when(jnp.logical_not(t_self))
    def _():
        pl.semaphore_signal(barrier, inc=1, device_id=(t_row, t_col), device_id_type=MESH)

    pl.semaphore_wait(barrier, rows + cols - 2 + jnp.where(t_self, 0, 1))

    def partner_copy():
        return pltpu.make_async_remote_copy(
            src_ref=child, dst_ref=partner, send_sem=p_s, recv_sem=p_r,
            device_id=(lax.rem(r + rows // 2, rows), c), device_id_type=MESH)

    def z_copy(i):
        return pltpu.make_async_remote_copy(
            src_ref=zin, dst_ref=zbuf.at[r], send_sem=z_s.at[i], recv_sem=z_r.at[i],
            device_id=(lax.rem(r + i + 1, rows), c), device_id_type=MESH)

    loop(rows - 1, lambda i: z_copy(i).start())
    partner_copy().start()
    zbuf[pl.ds(r, 1)] = zin[...][None]

    own8 = pl.ds(pl.multiple_of(r * 8, 8), 8)
    own16 = pl.ds(pl.multiple_of(c * 16, 16), 16)
    strip_c[:, own8, :] = scol[...]
    strip_r[:, own16, :] = srow[...]

    def plane_copy(a, src, dst, i):
        return pltpu.make_async_remote_copy(
            src_ref=src, dst_ref=dst, send_sem=plane_s.at[a, i], recv_sem=plane_r.at[a, i],
            device_id=(r, lax.rem(c + i + 1, cols)), device_id_type=MESH)

    def sr_copy(i):
        return plane_copy(0, srow, strip_r.at[:, own16, :], i)

    def d_copy(i):
        return plane_copy(1, dpiece, diag.at[:, own16, :], i)

    def vp_copy(i):
        return plane_copy(2, vpiece, vpiv.at[:, own16, :], i)

    def vr_copy(i):
        return plane_copy(3, placed, v_r.at[own16, :], i)

    loop(rows - 1, lambda i: z_copy(i).wait_recv())
    turned = jnp.transpose(zbuf[...].reshape(rows * 8, 128))
    dpiece[0] = turned[0:16]
    dpiece[1] = turned[16:32]
    dpiece[2] = turned[32:48]
    half = rows * 4

    def swapped_halves(x):
        return jnp.concatenate([x[:, half:], x[:, :half]], axis=1)

    vpiece[0] = (turned[64:80] + swapped_halves(turned[80:96])).astype(BF16)
    vpiece[1] = (turned[96:112] + swapped_halves(turned[112:128])).astype(BF16)
    diag[:, own16, :] = dpiece[...]
    vpiv[:, own16, :] = vpiece[...]
    loop(cols - 1, lambda i: d_copy(i).start())
    loop(cols - 1, lambda i: vp_copy(i).start())
    loop(cols - 1, lambda i: sr_copy(i).start())

    partner_copy().wait_recv()
    for j in range(MT // TS):
        total = jnp.zeros((16, TS), F32)
        for t in range(4):
            total = total + child[t].astype(F32) * pick[8 * j + t : 8 * j + t + 1, :]
            total = total + partner[t].astype(F32) * pick[8 * j + 4 + t : 8 * j + 5 + t, :]
        placed[:, j * TS : (j + 1) * TS] = total.astype(BF16)
    v_r[own16, :] = placed[...]

    def t_copy():
        return pltpu.make_async_remote_copy(
            src_ref=placed, dst_ref=v_c.at[t_row], send_sem=t_s, recv_sem=t_r,
            device_id=(t_row, t_col), device_id_type=MESH)

    @pl.when(t_self)
    def _():
        v_c[pl.ds(r, 1)] = placed[...][None]

    @pl.when(jnp.logical_not(t_self))
    def _():
        t_copy().start()

    loop(cols - 1, lambda i: vr_copy(i).start())

    @pl.when(jnp.logical_not(t_self))
    def _():
        t_copy().wait_recv()

    def slot(shift):
        return lax.rem(z + shift + chips, chips) * 2 + core

    def sc_piece(row):
        return strip_c.at[:, pl.ds(pl.multiple_of(row * 8, 8), 8), :]

    def ring_copy(a, way, s):
        sign = 1 - 2 * way
        row = slot(-sign * s)
        ref = sc_piece(row) if a == 0 else v_c.at[row]
        return pltpu.make_async_remote_copy(
            src_ref=ref, dst_ref=ref, send_sem=ring_s.at[a, way, s], recv_sem=ring_r.at[a, way, s],
            device_id=(slot(sign), c), device_id_type=MESH)

    def sib_copy(a, row):
        ref = sc_piece(row) if a == 0 else v_c.at[row]
        return pltpu.make_async_remote_copy(
            src_ref=ref, dst_ref=ref, send_sem=sib_s.at[a, row // 2], recv_sem=sib_r.at[a, row // 2],
            device_id=(2 * z + 1 - core, c), device_id_type=MESH)

    def ring_step(s):
        for a in range(2):
            ring_copy(a, 0, s).start()

            @pl.when(s < chips // 2 - 1)
            def _():
                ring_copy(a, 1, s).start()

            sib_copy(a, slot(-s)).start()

            @pl.when(s > 0)
            def _():
                sib_copy(a, slot(s)).start()

        for a in range(2):
            ring_copy(a, 0, s).wait_recv()

            @pl.when(s < chips // 2 - 1)
            def _():
                ring_copy(a, 1, s).wait_recv()

    loop(chips // 2, ring_step)
    for a in range(2):
        sib_copy(a, slot(chips // 2)).start()

    for copy in (sr_copy, d_copy, vp_copy, vr_copy):
        loop(cols - 1, lambda i: copy(i).wait_recv())
    for a in range(2):
        loop(chips, lambda i: sib_copy(a, 2 * i + core).wait_recv())
    loop(rows - 1, lambda i: z_copy(i).wait_send())
    partner_copy().wait_send()

    @pl.when(jnp.logical_not(t_self))
    def _():
        t_copy().wait_send()

    for copy in (sr_copy, d_copy, vp_copy, vr_copy):
        loop(cols - 1, lambda i: copy(i).wait_send())
    for a in range(2):
        loop(chips, lambda i: sib_copy(a, 2 * i + core).wait_send())
        loop(chips // 2, lambda s: ring_copy(a, 0, s).wait_send())
        loop(chips // 2 - 1, lambda s: ring_copy(a, 1, s).wait_send())


def gather(zin, srow, scol, child, pick, rows, cols):
    vmem = pl.BlockSpec(memory_space=pltpu.VMEM)
    dma = pltpu.SemaphoreType.DMA
    shape = jax.ShapeDtypeStruct
    width_r = srow.shape[2]
    width_c = scol.shape[2]
    return pl.pallas_call(
        comm_kernel,
        out_shape=(
            shape((3, PW, PW), F32),
            shape((2, PW, PW), BF16),
            shape((2, PW, width_r), F32),
            shape((2, PW, width_c), F32),
            shape((PW, width_r), BF16),
            shape((rows, 16, width_r), BF16),
        ),
        in_specs=[vmem] * 5,
        out_specs=(vmem,) * 6,
        scratch_shapes=[
            pltpu.VMEM((rows, 8, 128), F32),
            pltpu.VMEM((4, 16, TS), BF16),
            pltpu.VMEM((16, width_r), BF16),
            pltpu.VMEM((3, 16, PW), F32),
            pltpu.VMEM((2, 16, PW), BF16),
            dma((rows - 1,)), dma((rows - 1,)), dma, dma, dma, dma,
            dma((4, cols - 1)), dma((4, cols - 1)),
            dma((2, 2, rows // 4)), dma((2, 2, rows // 4)),
            dma((2, rows // 2)), dma((2, rows // 2)),
        ],
        compiler_params=pltpu.CompilerParams(
            collective_id=0, has_side_effects=True, vmem_limit_bytes=32 << 20),
    )(zin, srow, scol, child, pick)


def split3(x):
    high = x.astype(BF16)
    rest = x - high.astype(F32)
    mid = rest.astype(BF16)
    return high, mid, (rest - mid.astype(F32)).astype(BF16)


def dot6(a, b, ca, cb):
    ah, am, al = split3(a)
    bh, bm, bl = split3(b)
    left = jnp.concatenate([ah, ah, am, ah, al, am], axis=ca)
    right = jnp.concatenate([bh, bm, bh, bl, bh, bm], axis=cb)
    return lax.dot_general(left, right, (((ca,), (cb,)), ((), ())), preferred_element_type=F32)


def dot1(a, b, ca, cb):
    return lax.dot_general(a, b, (((ca,), (cb,)), ((), ())), preferred_element_type=F32)


def dot32(a, b):
    return lax.dot_general(
        a, b, (((1,), (0,)), ((), ())), precision=lax.Precision.HIGHEST, preferred_element_type=F32)


def block_inverse(block):
    ii = lax.broadcasted_iota(jnp.int32, (NB, 128), 0)
    ll = lax.broadcasted_iota(jnp.int32, (NB, 128), 1)
    m = jnp.where(ll < NB, block, jnp.where(ll == ii + NB, 1.0, 0.0).astype(F32))
    done = []
    for g in range(NB // SUB):
        low = SUB * g
        rows = [m[low + i : low + i + 1, :] for i in range(SUB)]
        s = {}
        for i in range(SUB):
            for k in range(i, SUB):
                s[i, k] = jnp.broadcast_to(rows[i][:, low + k : low + k + 1], (1, 128))
        for j in range(SUB):
            inv = lax.rsqrt(s[j, j])
            for k in range(j, SUB):
                s[j, k] = s[j, k] * inv
            rows[j] = rows[j] * inv
            for i in range(j + 1, SUB):
                for k in range(i, SUB):
                    s[i, k] = s[i, k] - s[j, i] * s[j, k]
                rows[i] = rows[i] - s[j, i] * rows[j]
        upper = jnp.concatenate(rows, axis=0)
        done.append(upper)
        if low + SUB < NB:
            across = jnp.transpose(jnp.concatenate([upper] * (128 // SUB), axis=0))
            for j in range(SUB):
                column = jnp.where(ii[:, 0:1] >= low + SUB, across[:NB, j : j + 1], 0.0)
                m = m - column * rows[j]
    return jnp.concatenate(done, axis=0)[:, NB : 2 * NB]


def factor(work):
    lane = lax.broadcasted_iota(jnp.int32, (NB, PW), 1)

    def step(b):
        here = pl.ds(pl.multiple_of(b * NB, NB), NB)
        band = work[here, :]
        lead = pltpu.roll(band[:, :PW], PW - b * NB, axis=1)
        inverse = block_inverse(lead[:, :128])
        upper = dot6(inverse, band, 1, 0)
        below = jnp.where(lane >= (b + 1) * NB, upper[:, :PW], 0.0)
        work[...] -= dot6(below, upper, 0, 0)
        work[here, :] = upper

    loop(PW // NB, step)


def panel_kernel(diag, vpiv, strip_r, strip_c, v_r, v_c, flags, out_a, out_b, work, wp, x0, x1, p01):
    i = lax.broadcasted_iota(jnp.int32, (PW, PW), 0)
    j = lax.broadcasted_iota(jnp.int32, (PW, PW), 1)
    eye = jnp.where(i == j, 1.0, 0.0).astype(F32)
    flag_p = flags[2:3, :PW].astype(BF16)
    for k in range(2):
        vp = vpiv[k]
        wp[k, PW:, :] = vp * flag_p
        wp[k, :PW, :] = vp - vp * flag_p
    work[:, :PW] = diag[0] + dot1(wp[0], wp[0], 0, 0)
    work[:, PW:] = eye
    factor(work)
    x0[...] = work[:, PW:]
    low = diag[1] + dot1(wp[1], wp[0], 0, 0)
    p01[...] = lax.dot_general(
        low, x0[...], (((1,), (1,)), ((), ())),
        precision=lax.Precision.HIGHEST, preferred_element_type=F32).astype(BF16)
    work[:, :PW] = diag[2] + dot1(wp[1], wp[1], 0, 0) - dot1(p01[...], p01[...], 1, 1)
    work[:, PW:] = eye
    factor(work)
    x1[...] = work[:, PW:]

    def tile(strip, v, flag, out, lanes, at, sign):
        flag = flag.astype(BF16)
        top = v - v * flag
        bottom = v * flag
        out[0:PW, at] = top
        out[PW : 2 * PW, at] = bottom
        w = jnp.concatenate([top, bottom], axis=0)
        s0 = strip[0, :, at] + dot1(wp[0], w, 0, 0)
        first = dot32(x0[...], s0).astype(BF16)
        out[2 * PW : 3 * PW, at] = first * sign
        s1 = strip[1, :, at] + dot1(wp[1], w, 0, 0) - dot1(p01[...], first, 1, 0)
        second = dot32(x1[...], s1).astype(BF16)
        out[3 * PW : 4 * PW, at] = second * sign

    rows_wide = v_r.shape[1]
    for h in range(rows_wide // PW):
        at = slice(h * PW, (h + 1) * PW)
        tile(strip_r, v_r[:, at], flags[1:2, at], out_a, PW, at, BF16(1))
    half = v_c.shape[0]
    for q in range(2):
        for h in range(rows_wide // PW):
            sub = slice(h * PW, (h + 1) * PW)
            at = slice(q * rows_wide + h * PW, q * rows_wide + (h + 1) * PW)
            v = v_c[:, q, :, sub].reshape(half * 16, PW)
            tile(strip_c, v, flags[0:1, at], out_b, PW, at, BF16(-1))


def panels(diag, vpiv, strip_r, strip_c, v_r, v_c, flags):
    vmem = pl.BlockSpec(memory_space=pltpu.VMEM)
    shape = jax.ShapeDtypeStruct
    v_c = v_c.reshape(v_c.shape[0] // 2, 2, 16, v_c.shape[2])
    return pl.pallas_call(
        panel_kernel,
        out_shape=(shape((4 * PW, strip_r.shape[2]), BF16), shape((4 * PW, strip_c.shape[2]), BF16)),
        in_specs=[vmem] * 7,
        out_specs=(vmem, vmem),
        scratch_shapes=[
            pltpu.VMEM((PW, 2 * PW), F32),
            pltpu.VMEM((2, 2 * PW, PW), BF16),
            pltpu.VMEM((PW, PW), F32),
            pltpu.VMEM((PW, PW), F32),
            pltpu.VMEM((PW, PW), BF16),
        ],
        compiler_params=pltpu.CompilerParams(vmem_limit_bytes=40 << 20),
    )(diag, vpiv, strip_r, strip_c, v_r, v_c, flags)


def final_kernel(front, left, right, scale, schur, panel):
    g = pl.program_id(0)
    r = lax.axis_index("row")
    c = lax.axis_index("col")
    rows, wide = schur.shape
    ii = lax.broadcasted_iota(jnp.int32, (rows, wide), 0)
    jj = lax.rem(lax.broadcasted_iota(jnp.int32, (rows, wide), 1) + g * wide, MT)
    keep = jnp.logical_and(ii >= 16, jj >= 16)
    total = front[...] * scale[0:1, :] + dot1(left[...], right[...], 0, 0)
    schur[...] = jnp.where(keep, total, 0.0)

    @pl.when(g == 0)
    def _():
        at = pl.multiple_of(c * 16, 16)
        m = lax.broadcasted_iota(jnp.int32, (16, rows), 0) + c * 16
        a = lax.broadcasted_iota(jnp.int32, (16, rows), 1)
        p0 = left[pl.ds(2 * PW + at, 16), :].astype(F32)
        p1 = left[pl.ds(3 * PW + at, 16), :].astype(F32)
        p0 = jnp.where(jnp.logical_or(a >= 8, m <= r * 8 + a), p0, 0.0)
        p1 = jnp.where(jnp.logical_or(a >= 16, m <= r * 8 + a - 8), p1, 0.0)
        p1 = jnp.where(a >= 8, p1, 0.0)
        panel[...] = jnp.transpose(jnp.concatenate([p0, p1], axis=0)).astype(BF16)


def final(front, left, right, scale):
    rows, wide = front.shape
    step = 256
    return pl.pallas_call(
        final_kernel,
        grid=(wide // step,),
        out_shape=(
            jax.ShapeDtypeStruct((rows, wide), F32),
            jax.ShapeDtypeStruct((rows, 32), BF16),
        ),
        in_specs=[
            pl.BlockSpec((rows, step), lambda g: (0, g)),
            pl.BlockSpec((4 * PW, rows), lambda g: (0, 0)),
            pl.BlockSpec((4 * PW, step), lambda g: (0, g)),
            pl.BlockSpec((8, step), lambda g: (0, g)),
        ],
        out_specs=(
            pl.BlockSpec((rows, step), lambda g: (0, g)),
            pl.BlockSpec((rows, 32), lambda g: (0, 0)),
        ),
        compiler_params=pltpu.CompilerParams(vmem_limit_bytes=32 << 20),
    )(front, left, right, scale)


def local(front, tile_group, child, row_map):
    rows = lax.axis_size("row")
    cols = lax.axis_size("col")
    r = lax.axis_index("row")
    c = lax.axis_index("col")
    height, width = front.shape
    tiles = height // TS
    group_r = lax.dynamic_slice_in_dim(tile_group, r, 1)
    group_c = lax.dynamic_slice_in_dim(tile_group, 2 * c, 2)
    same = (group_r == group_c).astype(F32)
    scale = jnp.broadcast_to(jnp.repeat(same, MT)[None, :], (8, width))

    wide = front.reshape(height, 2, MT)[:, :, :16].reshape(height, 2, 2, 8) * same[None, :, None, None]
    srow = wide.transpose(2, 1, 3, 0).reshape(2, 16, height)
    scol = (front[:16] * scale[0:1]).reshape(2, 8, width)

    own_map = lax.dynamic_slice_in_dim(row_map, r * tiles, tiles)
    other = jnp.bitwise_xor(r, rows // 2)
    partner_map = lax.dynamic_slice_in_dim(row_map, other * tiles, tiles)
    both = jnp.concatenate([own_map, partner_map])
    pick = (both[None, :] == (r * tiles + jnp.arange(tiles, dtype=jnp.int32))[:, None]).astype(F32)
    pick = jnp.broadcast_to(pick.reshape(8 * tiles, 1), (8 * tiles, TS))

    corner = wide[:16].reshape(2, 8, 2, 2, 8)
    heads = child.reshape(tiles, TS, 16)[:, :16].astype(F32)
    parts = []
    for target in (r, other):
        chosen = (own_map == target * tiles).astype(F32)
        parts.append(jnp.sum(heads * chosen[:, None, None], axis=0).reshape(2, 8, 16))
    zin = jnp.concatenate(
        [
            corner[0, :, :, 0, :].reshape(8, 16),
            corner[0, :, :, 1, :].reshape(8, 16),
            corner[1, :, :, 1, :].reshape(8, 16),
            jnp.zeros((8, 16), F32),
            parts[0][0], parts[1][0], parts[0][1], parts[1][1],
        ],
        axis=1,
    )

    count = row_map.shape[0]
    second = (row_map[count // 2 :, None] == jnp.arange(count, dtype=jnp.int32)[None, :]).any(axis=0)
    second = second.astype(F32)
    flag_c = jnp.repeat(lax.dynamic_slice_in_dim(second, 2 * c * tiles, 2 * tiles), TS)
    flag_r = jnp.repeat(lax.dynamic_slice_in_dim(second, r * tiles, tiles), TS)
    flag_p = jnp.repeat(second[::tiles], 8)
    flags = jnp.stack([
        flag_c,
        jnp.concatenate([flag_r, jnp.zeros((width - height,), F32)]),
        jnp.concatenate([flag_p, jnp.zeros((width - PW,), F32)]),
    ])
    flags = jnp.concatenate([flags, jnp.zeros((5, width), F32)])

    child_t = child.reshape(tiles, TS, 16).transpose(0, 2, 1)
    gathered = gather(zin, srow, scol, child_t, pick, rows, cols)
    left, right = panels(*gathered, flags)
    schur, panel = final(front, left, right, scale)
    return panel, schur


def solution(mesh):
    placed = (P("row", "col"), P(), P("row", "col"), P())
    return jax.shard_map(
        local,
        mesh=mesh,
        in_specs=placed,
        out_specs=(P("row", "col"), P("row", "col")),
        check_vma=False,
    )
```

```python
import functools

import jax
import jax.numpy as jnp
from jax import lax
from jax.experimental import pallas as pl
from jax.experimental.pallas import tpu as pltpu
from jax.sharding import PartitionSpec as P

PW = 256
NP = 2
TS = 128
MT = 512
NB = 32
SUB = 8
F32 = jnp.float32
BF16 = jnp.bfloat16
MESH = pl.DeviceIdType.MESH


def loop(count, body):
    def step(i, carry):
        body(i)
        return carry

    lax.fori_loop(0, count, step, 0)


def split3(x):
    high = x.astype(BF16)
    rest = x - high.astype(F32)
    mid = rest.astype(BF16)
    return high, mid, (rest - mid.astype(F32)).astype(BF16)


def dot6(a, b, ca, cb):
    ah, am, al = split3(a)
    bh, bm, bl = split3(b)
    left = jnp.concatenate([ah, ah, am, ah, al, am], axis=ca)
    right = jnp.concatenate([bh, bm, bh, bl, bh, bm], axis=cb)
    return lax.dot_general(left, right, (((ca,), (cb,)), ((), ())), preferred_element_type=F32)


def dot1(a, b, ca, cb):
    return lax.dot_general(a, b, (((ca,), (cb,)), ((), ())), preferred_element_type=F32)


def block_inverse(block):
    ii = lax.broadcasted_iota(jnp.int32, (NB, 128), 0)
    ll = lax.broadcasted_iota(jnp.int32, (NB, 128), 1)
    m = jnp.where(ll < NB, block, jnp.where(ll == ii + NB, 1.0, 0.0).astype(F32))
    done = []
    for g in range(NB // SUB):
        low = SUB * g
        rows = [m[low + i : low + i + 1, :] for i in range(SUB)]
        s = {}
        for i in range(SUB):
            for k in range(i, SUB):
                s[i, k] = jnp.broadcast_to(rows[i][:, low + k : low + k + 1], (1, 128))
        for j in range(SUB):
            inv = lax.rsqrt(s[j, j])
            for k in range(j, SUB):
                s[j, k] = s[j, k] * inv
            rows[j] = rows[j] * inv
            for i in range(j + 1, SUB):
                for k in range(i, SUB):
                    s[i, k] = s[i, k] - s[j, i] * s[j, k]
                rows[i] = rows[i] - s[j, i] * rows[j]
        upper = jnp.concatenate(rows, axis=0)
        done.append(upper)
        if low + SUB < NB:
            across = jnp.transpose(jnp.concatenate([upper] * (128 // SUB), axis=0))
            for j in range(SUB):
                column = jnp.where(ii[:, 0:1] >= low + SUB, across[:NB, j : j + 1], 0.0)
                m = m - column * rows[j]
    return jnp.concatenate(done, axis=0)[:, NB : 2 * NB]


def factor(work, beside):
    lane = lax.broadcasted_iota(jnp.int32, (NB, PW), 1)

    def step(b):
        beside(b)
        here = pl.ds(pl.multiple_of(b * NB, NB), NB)
        band = work[here, :]
        lead = pltpu.roll(band[:, :PW], PW - b * NB, axis=1)
        inverse = block_inverse(lead[:, :128])
        upper = dot6(inverse, band, 1, 0)
        below = jnp.where(lane >= (b + 1) * NB, upper[:, :PW], 0.0)
        work[...] -= dot6(below, upper, 0, 0)
        work[here, :] = upper

    loop(PW // NB, step)


def split2(x, axis):
    high = x.astype(BF16)
    low = (x - high.astype(F32)).astype(BF16)
    return high, low


def left3(x):
    high, low = split2(x, 1)
    return jnp.concatenate([high, high, low], axis=1)


def right3(x, axis):
    high, low = split2(x, axis)
    return jnp.concatenate([high, low, high], axis=axis)


def front_kernel(
    front, child, groups, tile_map, map_lanes,
    out_a, out_b,
    zin, srow, zbuf, partner, placed, dpiece, vpiece,
    diag, vpiv, strip_r, strip_c, v_r, v_c, flags,
    work, wp, x0, x1, p01,
    z_s, z_r, p_s, p_r, t_s, t_r,
    plane_s, plane_r, ring_s, ring_r, sib_s, sib_r,
):
    r = lax.axis_index("row")
    c = lax.axis_index("col")
    rows = lax.axis_size("row")
    cols = lax.axis_size("col")
    height, width = front.shape
    z = r // 2
    core = r % 2
    chips = rows // 2
    other = lax.rem(r + chips, rows)
    t_row = 2 * c + core
    t_col = z
    t_self = jnp.logical_and(t_row == r, t_col == c)

    barrier = pltpu.get_barrier_semaphore()

    def hello_row(i):
        pl.semaphore_signal(barrier, inc=1, device_id=(lax.rem(r + i + 1, rows), c), device_id_type=MESH)

    def hello_col(i):
        pl.semaphore_signal(barrier, inc=1, device_id=(r, lax.rem(c + i + 1, cols)), device_id_type=MESH)

    loop(rows - 1, hello_row)
    loop(cols - 1, hello_col)

    @pl.when(jnp.logical_not(t_self))
    def _():
        pl.semaphore_signal(barrier, inc=1, device_id=(t_row, t_col), device_id_type=MESH)

    def one_if(same):
        return jnp.where(same, 1.0, 0.0).astype(F32)

    coupled = [one_if(groups[r] == groups[2 * c + q]) for q in range(2)]
    turned = []
    for q in range(2):
        t = jnp.transpose(front[:, q * MT : q * MT + 128])[:16] * coupled[q]
        srow[0, 8 * q : 8 * q + 8, :] = t[:8]
        srow[1, 8 * q : 8 * q + 8, :] = t[8:]
        turned.append(t[:, :128])
    own_maps = [tile_map[4 * r + t] for t in range(4)]
    other_maps = [tile_map[4 * other + t] for t in range(4)]
    heads = []
    for target in (r, other):
        total = jnp.zeros((16, TS), F32)
        for t in range(4):
            total = total + child[:, t * TS : (t + 1) * TS].astype(F32) * one_if(own_maps[t] == 4 * target)
        heads.append(total)

    def second8(x):
        return pltpu.roll(x, 120, axis=1)

    tall = jnp.concatenate(
        [
            turned[0][:8], turned[1][:8], turned[0][8:], turned[1][8:],
            second8(turned[0])[8:], second8(turned[1])[8:], jnp.zeros((16, 128), F32),
            heads[0], heads[1], second8(heads[0]), second8(heads[1]),
        ],
        axis=0,
    )
    zin[...] = jnp.transpose(tall)[:8]

    pl.semaphore_wait(barrier, rows + cols - 2 + jnp.where(t_self, 0, 1))

    def z_copy(i):
        return pltpu.make_async_remote_copy(
            src_ref=zin, dst_ref=zbuf.at[r], send_sem=z_s.at[i], recv_sem=z_r.at[i],
            device_id=(lax.rem(r + i + 1, rows), c), device_id_type=MESH)

    def partner_copy():
        return pltpu.make_async_remote_copy(
            src_ref=child, dst_ref=partner, send_sem=p_s, recv_sem=p_r,
            device_id=(other, c), device_id_type=MESH)

    loop(rows - 1, lambda i: z_copy(i).start())
    partner_copy().start()
    zbuf[pl.ds(r, 1)] = zin[...][None]

    own8 = pl.ds(pl.multiple_of(r * 8, 8), 8)
    own16 = pl.ds(pl.multiple_of(c * 16, 16), 16)
    for k in range(2):
        for q in range(2):
            strip_c[k, own8, q * MT : (q + 1) * MT] = (
                front[8 * k : 8 * k + 8, q * MT : (q + 1) * MT] * coupled[q])
    strip_r[:, own16, :] = srow[...]

    listed = jnp.transpose(jnp.broadcast_to(map_lanes[...].astype(F32), (128, 128)))
    count = map_lanes.shape[1]
    at_lane = lax.broadcasted_iota(jnp.int32, (128, 128), 1).astype(F32)
    child_id = lax.broadcasted_iota(jnp.int32, (128, 128), 0)
    hits = jnp.where(jnp.logical_and(listed == at_lane, child_id >= count // 2), 1.0, 0.0)
    second = jnp.broadcast_to(jnp.sum(hits, axis=0, keepdims=True), (8, 128)).astype(BF16)

    def spread(tile_of_lane, lanes):
        tile = lax.broadcasted_iota(jnp.int32, (128, lanes), 0)
        lane = lax.broadcasted_iota(jnp.int32, (128, lanes), 1)
        chosen = jnp.where(tile == tile_of_lane(lane), 1.0, 0.0).astype(BF16)
        return dot1(second, chosen, 1, 0).astype(BF16)

    flag_p = spread(lambda lane: 4 * lax.shift_right_logical(lane, 3), PW)[0:1]
    flags[0:8, :height] = spread(lambda lane: 4 * r + lax.shift_right_logical(lane, 7), height).astype(F32)
    flags[0:8, height:] = spread(lambda lane: 8 * c + lax.shift_right_logical(lane, 7), width).astype(F32)

    def plane_copy(a, src, dst, i):
        return pltpu.make_async_remote_copy(
            src_ref=src, dst_ref=dst, send_sem=plane_s.at[a, i], recv_sem=plane_r.at[a, i],
            device_id=(r, lax.rem(c + i + 1, cols)), device_id_type=MESH)

    def sr_copy(i):
        return plane_copy(0, srow, strip_r.at[:, own16, :], i)

    def d_copy(i):
        return plane_copy(1, dpiece.at[0], diag.at[0, own16, :], i)

    def d1_copy(i):
        return plane_copy(4, dpiece.at[pl.ds(1, 2)], diag.at[pl.ds(1, 2), own16, :], i)

    def vp_copy(i):
        return plane_copy(2, vpiece, vpiv.at[:, own16, :], i)

    def vr_copy(i):
        return plane_copy(3, placed, v_r.at[own16, :], i)

    loop(rows - 1, lambda i: z_copy(i).wait_recv())
    flat = jnp.transpose(zbuf[...].reshape(rows * 8, 128))
    dpiece[0] = flat[0:16]
    dpiece[1] = flat[16:32]
    dpiece[2] = flat[32:48]
    half = rows * 4

    def swapped_halves(x):
        return jnp.concatenate([x[:, half:], x[:, :half]], axis=1)

    vpiece[0] = (flat[64:80] + swapped_halves(flat[80:96])).astype(BF16)
    vpiece[1] = (flat[96:112] + swapped_halves(flat[112:128])).astype(BF16)
    diag[:, own16, :] = dpiece[...]
    vpiv[:, own16, :] = vpiece[...]
    loop(cols - 1, lambda i: vp_copy(i).start())
    loop(cols - 1, lambda i: d_copy(i).start())
    loop(cols - 1, lambda i: d1_copy(i).start())

    partner_copy().wait_recv()
    for j in range(height // TS):
        total = jnp.zeros((16, TS), F32)
        for t in range(4):
            at = slice(t * TS, (t + 1) * TS)
            total = total + child[:, at].astype(F32) * one_if(own_maps[t] == 4 * r + j)
            total = total + partner[:, at].astype(F32) * one_if(other_maps[t] == 4 * r + j)
        placed[:, j * TS : (j + 1) * TS] = total.astype(BF16)
    v_r[own16, :] = placed[...]

    def t_copy():
        return pltpu.make_async_remote_copy(
            src_ref=placed, dst_ref=v_c.at[t_row], send_sem=t_s, recv_sem=t_r,
            device_id=(t_row, t_col), device_id_type=MESH)

    @pl.when(t_self)
    def _():
        v_c[pl.ds(r, 1)] = placed[...][None]

    @pl.when(jnp.logical_not(t_self))
    def _():
        t_copy().start()

    loop(cols - 1, lambda i: vr_copy(i).start())
    loop(cols - 1, lambda i: sr_copy(i).start())

    @pl.when(jnp.logical_not(t_self))
    def _():
        t_copy().wait_recv()

    def slot(shift):
        return lax.rem(z + shift + chips, chips) * 2 + core

    def piece(a, row):
        if a == 0:
            return strip_c.at[:, pl.ds(pl.multiple_of(row * 8, 8), 8), :]
        return v_c.at[row]

    def ring_copy(a, way, s):
        sign = 1 - 2 * way
        ref = piece(a, slot(-sign * s))
        return pltpu.make_async_remote_copy(
            src_ref=ref, dst_ref=ref, send_sem=ring_s.at[a, way, s], recv_sem=ring_r.at[a, way, s],
            device_id=(slot(sign), c), device_id_type=MESH)

    def sib_copy(a, row):
        ref = piece(a, row)
        return pltpu.make_async_remote_copy(
            src_ref=ref, dst_ref=ref, send_sem=sib_s.at[a, row // 2], recv_sem=sib_r.at[a, row // 2],
            device_id=(2 * z + 1 - core, c), device_id_type=MESH)

    hops = chips // 2

    def ring_start(s):
        for a in range(2):
            ring_copy(a, 0, s).start()

            @pl.when(s < hops - 1)
            def _():
                ring_copy(a, 1, s).start()

            sib_copy(a, slot(-s)).start()

            @pl.when(s > 0)
            def _():
                sib_copy(a, slot(s)).start()

    def ring_wait(s):
        for a in range(2):
            ring_copy(a, 0, s).wait_recv()

            @pl.when(s < hops - 1)
            def _():
                ring_copy(a, 1, s).wait_recv()

    ring_start(0)

    def ring_beside(first):
        def beside(b):
            s = first + b // 2

            @pl.when(b % 2 == 1)
            def _():
                ring_wait(s)

                @pl.when(s < hops - 1)
                def _():
                    ring_start(s + 1)

        return beside

    loop(cols - 1, lambda i: vp_copy(i).wait_recv())
    for k in range(2):
        vp = vpiv[k]
        wp[k, PW:, :] = vp * flag_p
        wp[k, :PW, :] = vp - vp * flag_p
    i = lax.broadcasted_iota(jnp.int32, (PW, PW), 0)
    j = lax.broadcasted_iota(jnp.int32, (PW, PW), 1)
    eye = jnp.where(i == j, 1.0, 0.0).astype(F32)
    outer = dot1(wp[0], wp[0], 0, 0)
    loop(cols - 1, lambda i: d_copy(i).wait_recv())
    work[:, :PW] = diag[0] + outer
    work[:, PW:] = eye
    factor(work, ring_beside(0))
    x0[...] = left3(work[:, PW:])
    loop(cols - 1, lambda i: d1_copy(i).wait_recv())
    low = diag[1] + dot1(wp[1], wp[0], 0, 0)
    p01[...] = dot1(right3(low, 1), x0[...], 1, 1).astype(BF16)

    work[:, :PW] = diag[2] + dot1(wp[1], wp[1], 0, 0) - dot1(p01[...], p01[...], 1, 1)
    work[:, PW:] = eye
    factor(work, ring_beside(hops // 2))
    x1[...] = left3(work[:, PW:])
    for a in range(2):
        sib_copy(a, slot(hops)).start()

    for copy in (sr_copy, vr_copy):
        loop(cols - 1, lambda i: copy(i).wait_recv())

    def tile(strip, v, flag, out, at, sign):
        flag = flag.astype(BF16)
        bottom = v * flag
        top = v - bottom
        out[0:PW, at] = top
        out[PW : 2 * PW, at] = bottom
        w = jnp.concatenate([top, bottom], axis=0)
        s0 = strip[0, :, at] + dot1(wp[0], w, 0, 0)
        first = dot1(x0[...], right3(s0, 0), 1, 0).astype(BF16)
        out[2 * PW : 3 * PW, at] = first * sign
        s1 = strip[1, :, at] + dot1(wp[1], w, 0, 0) - dot1(p01[...], first, 1, 0)
        second = dot1(x1[...], right3(s1, 0), 1, 0).astype(BF16)
        out[3 * PW : 4 * PW, at] = second * sign

    for h in range(height // PW):
        at = slice(h * PW, (h + 1) * PW)
        tile(strip_r, v_r[:, at], flags[0:1, at], out_a, at, BF16(1))
    for a in range(2):
        loop(chips, lambda i: sib_copy(a, 2 * i + core).wait_recv())
    for q in range(2):
        for h in range(height // PW):
            sub = slice(h * PW, (h + 1) * PW)
            at = slice(q * height + h * PW, q * height + (h + 1) * PW)
            v = jnp.concatenate([v_c[2 * i + q, :, sub] for i in range(chips)], axis=0)
            lanes = slice(height + at.start, height + at.stop)
            tile(strip_c, v, flags[0:1, lanes], out_b, at, BF16(-1))

    loop(rows - 1, lambda i: z_copy(i).wait_send())
    partner_copy().wait_send()

    @pl.when(jnp.logical_not(t_self))
    def _():
        t_copy().wait_send()

    for copy in (sr_copy, d_copy, d1_copy, vp_copy, vr_copy):
        loop(cols - 1, lambda i: copy(i).wait_send())
    for a in range(2):
        loop(chips, lambda i: sib_copy(a, 2 * i + core).wait_send())
        loop(hops, lambda s: ring_copy(a, 0, s).wait_send())
        loop(hops - 1, lambda s: ring_copy(a, 1, s).wait_send())


def panels(front, child, tile_group, row_map, rows, cols):
    vmem = pl.BlockSpec(memory_space=pltpu.VMEM)
    smem = pl.BlockSpec(memory_space=pltpu.SMEM)
    dma = pltpu.SemaphoreType.DMA
    shape = jax.ShapeDtypeStruct
    height, width = front.shape
    return pl.pallas_call(
        front_kernel,
        out_shape=(shape((4 * PW, height), BF16), shape((4 * PW, width), BF16)),
        in_specs=[vmem, vmem, smem, smem, vmem],
        out_specs=(vmem, vmem),
        scratch_shapes=[
            pltpu.VMEM((8, 128), F32),
            pltpu.VMEM((2, 16, height), F32),
            pltpu.VMEM((rows, 8, 128), F32),
            pltpu.VMEM((16, height), BF16),
            pltpu.VMEM((16, height), BF16),
            pltpu.VMEM((3, 16, PW), F32),
            pltpu.VMEM((2, 16, PW), BF16),
            pltpu.VMEM((3, PW, PW), F32),
            pltpu.VMEM((2, PW, PW), BF16),
            pltpu.VMEM((2, PW, height), F32),
            pltpu.VMEM((2, PW, width), F32),
            pltpu.VMEM((PW, height), BF16),
            pltpu.VMEM((rows, 16, height), BF16),
            pltpu.VMEM((8, height + width), F32),
            pltpu.VMEM((PW, 2 * PW), F32),
            pltpu.VMEM((2, 2 * PW, PW), BF16),
            pltpu.VMEM((PW, 3 * PW), BF16),
            pltpu.VMEM((PW, 3 * PW), BF16),
            pltpu.VMEM((PW, PW), BF16),
            dma((rows - 1,)), dma((rows - 1,)), dma, dma, dma, dma,
            dma((5, cols - 1)), dma((5, cols - 1)),
            dma((2, 2, rows // 4)), dma((2, 2, rows // 4)),
            dma((2, rows // 2)), dma((2, rows // 2)),
        ],
        compiler_params=pltpu.CompilerParams(
            collective_id=0, has_side_effects=True, vmem_limit_bytes=40 << 20),
    )(front, child, tile_group, row_map, row_map.reshape(1, -1))


def final_kernel(front, left, right, groups, schur, panel):
    g = pl.program_id(0)
    r = lax.axis_index("row")
    c = lax.axis_index("col")
    rows, wide = schur.shape
    ii = lax.broadcasted_iota(jnp.int32, (rows, wide), 0)
    jj = lax.rem(lax.broadcasted_iota(jnp.int32, (rows, wide), 1) + g * wide, MT)
    keep = jnp.logical_and(ii >= 16, jj >= 16)
    coupled = jnp.where(groups[r] == groups[2 * c + (g * wide) // MT], 1.0, 0.0).astype(F32)
    total = front[...] * coupled + dot1(left[...], right[...], 0, 0)
    schur[...] = jnp.where(keep, total, 0.0)

    @pl.when(g == 0)
    def _():
        at = pl.multiple_of(c * 16, 16)
        m = lax.broadcasted_iota(jnp.int32, (16, rows), 0) + c * 16
        a = lax.broadcasted_iota(jnp.int32, (16, rows), 1)
        p0 = left[pl.ds(2 * PW + at, 16), :].astype(F32)
        p1 = left[pl.ds(3 * PW + at, 16), :].astype(F32)
        p0 = jnp.where(jnp.logical_or(a >= 8, m <= r * 8 + a), p0, 0.0)
        p1 = jnp.where(jnp.logical_or(a >= 16, m <= r * 8 + a - 8), p1, 0.0)
        p1 = jnp.where(a >= 8, p1, 0.0)
        panel[0:16, :] = p0.astype(BF16)
        panel[16:32, :] = p1.astype(BF16)


def final(front, left, right, tile_group):
    rows, wide = front.shape
    step = 256
    return pl.pallas_call(
        final_kernel,
        grid=(wide // step,),
        out_shape=(
            jax.ShapeDtypeStruct((rows, wide), F32),
            jax.ShapeDtypeStruct((32, rows), BF16),
        ),
        in_specs=[
            pl.BlockSpec((rows, step), lambda g: (0, g)),
            pl.BlockSpec((4 * PW, rows), lambda g: (0, 0)),
            pl.BlockSpec((4 * PW, step), lambda g: (0, g)),
            pl.BlockSpec(memory_space=pltpu.SMEM),
        ],
        out_specs=(
            pl.BlockSpec((rows, step), lambda g: (0, g)),
            pl.BlockSpec((32, rows), lambda g: (0, 0)),
        ),
        compiler_params=pltpu.CompilerParams(vmem_limit_bytes=32 << 20),
    )(front, left, right, tile_group)


def local(front, tile_group, child, row_map):
    rows = lax.axis_size("row")
    cols = lax.axis_size("col")
    left, right = panels(front, child.T, tile_group, row_map, rows, cols)
    schur, panel = final(front, left, right, tile_group)
    return panel.T, schur


def solution(mesh):
    placed = (P("row", "col"), P(), P("row", "col"), P())
    return jax.shard_map(
        local,
        mesh=mesh,
        in_specs=placed,
        out_specs=(P("row", "col"), P("row", "col")),
        check_vma=False,
    )
```

```python
import functools

import jax
import jax.numpy as jnp
from jax import lax
from jax.experimental import pallas as pl
from jax.experimental.pallas import tpu as pltpu
from jax.sharding import PartitionSpec as P

PW = 256
NP = 2
TS = 128
MT = 512
NB = 64
F32 = jnp.float32
BF16 = jnp.bfloat16
MESH = pl.DeviceIdType.MESH


def loop(count, body):
    def step(i, carry):
        body(i)
        return carry

    lax.fori_loop(0, count, step, 0)


def split3(x):
    high = x.astype(BF16)
    rest = x - high.astype(F32)
    mid = rest.astype(BF16)
    return high, mid, (rest - mid.astype(F32)).astype(BF16)


def dot6(a, b, ca, cb):
    ah, am, al = split3(a)
    bh, bm, bl = split3(b)
    left = jnp.concatenate([ah, ah, am, ah, al, am], axis=ca)
    right = jnp.concatenate([bh, bm, bh, bl, bh, bm], axis=cb)
    return lax.dot_general(left, right, (((ca,), (cb,)), ((), ())), preferred_element_type=F32)


def dot1(a, b, ca, cb):
    return lax.dot_general(a, b, (((ca,), (cb,)), ((), ())), preferred_element_type=F32)


def block_inverse(block):
    ii = lax.broadcasted_iota(jnp.int32, (8, 128), 0)
    ll = lax.broadcasted_iota(jnp.int32, (8, 128), 1)
    groups = NB // 8
    m = []
    for g in range(groups):
        unit = jnp.where(ll == ii + (8 * g + NB), 1.0, 0.0).astype(F32)
        m.append(jnp.where(ll < NB, block[8 * g : 8 * g + 8, :], unit))
    for g in range(groups):
        low = 8 * g
        rest = range(g + 1, groups)
        rows = [jnp.broadcast_to(m[g][i : i + 1, :], (8, 128)) for i in range(8)]
        s = {}
        for i in range(8):
            for k in range(i, 8):
                s[i, k] = jnp.broadcast_to(rows[i][:, low + k : low + k + 1], (8, 128))
        cols = {}
        for h in rest:
            for k in range(8):
                cols[h, k] = jnp.broadcast_to(m[h][:, low + k : low + k + 1], (8, 128))
        for j in range(8):
            inv = lax.rsqrt(s[j, j])
            for k in range(j + 1, 8):
                s[j, k] = s[j, k] * inv
            for i in range(j + 1, 8):
                for k in range(i, 8):
                    s[i, k] = s[i, k] - s[j, i] * s[j, k]
            rows[j] = rows[j] * inv
            for i in range(j + 1, 8):
                rows[i] = rows[i] - s[j, i] * rows[j]
            for h in rest:
                cols[h, j] = cols[h, j] * inv
                for i in range(j + 1, 8):
                    cols[h, i] = cols[h, i] - s[j, i] * cols[h, j]
        merged = rows[0]
        for i in range(1, 8):
            merged = jnp.where(ii == i, rows[i], merged)
        m[g] = merged
        for h in rest:
            for j in range(8):
                m[h] = m[h] - cols[h, j] * rows[j]
    return jnp.concatenate(m, axis=0)[:, NB : 2 * NB]


def factor(work, beside):
    lane = lax.broadcasted_iota(jnp.int32, (NB, PW), 1)

    def step(b):
        beside(2 * b)
        here = pl.ds(pl.multiple_of(b * NB, NB), NB)
        band = work[here, :]
        lead = pltpu.roll(band[:, :PW], PW - b * NB, axis=1)
        inverse = block_inverse(lead[:, :128])
        beside(2 * b + 1)
        upper = dot6(inverse, band, 1, 0)
        below = jnp.where(lane >= (b + 1) * NB, upper[:, :PW], 0.0)
        work[...] -= dot6(below, upper, 0, 0)
        work[here, :] = upper

    loop(PW // NB, step)


def split2(x, axis):
    high = x.astype(BF16)
    low = (x - high.astype(F32)).astype(BF16)
    return high, low


def left3(x):
    high, low = split2(x, 1)
    return jnp.concatenate([high, high, low], axis=1)


def right3(x, axis):
    high, low = split2(x, axis)
    return jnp.concatenate([high, low, high], axis=axis)


def front_kernel(
    front_hbm, child_hbm, groups_hbm, map_hbm, lanes_hbm,
    out_a, out_b,
    fcols, frows, child, groups, tile_map, map_lanes, in_s,
    zin, srow, zbuf, partner, placed, dpiece, vpiece,
    diag, vpiv, strip_r, strip_c, v_r, v_c, flags,
    work, wp, x0, x1, p01,
    z_s, z_r, p_s, p_r, t_s, t_r,
    plane_s, plane_r, ring_s, ring_r, sib_s, sib_r,
):
    r = lax.axis_index("row")
    c = lax.axis_index("col")
    rows = lax.axis_size("row")
    cols = lax.axis_size("col")
    height, width = front_hbm.shape
    z = r // 2
    core = r % 2
    chips = rows // 2
    other = lax.rem(r + chips, rows)
    t_row = 2 * c + core
    t_col = z
    t_self = jnp.logical_and(t_row == r, t_col == c)

    barrier = pltpu.get_barrier_semaphore()

    loads = [
        pltpu.make_async_copy(src, dst, in_s.at[i])
        for i, (src, dst) in enumerate([
            (front_hbm.at[:, pl.ds(0, 128)], fcols.at[0]),
            (front_hbm.at[:, pl.ds(MT, 128)], fcols.at[1]),
            (child_hbm, child),
            (groups_hbm, groups),
            (map_hbm, tile_map),
            (front_hbm.at[pl.ds(0, 16), :], frows),
            (lanes_hbm, map_lanes),
        ])
    ]
    for load in loads:
        load.start()

    def hello(row, col):
        pl.semaphore_signal(barrier, inc=1, device_id=(row, col), device_id_type=MESH)

    loop(chips - 1, lambda i: hello(lax.rem(r + 2 * i + 2, rows), c))
    loop(cols - 1, lambda i: hello(r, lax.rem(c + i + 1, cols)))
    hello(2 * z + 1 - core, c)

    @pl.when(jnp.logical_not(t_self))
    def _():
        pl.semaphore_signal(barrier, inc=1, device_id=(t_row, t_col), device_id_type=MESH)

    def one_if(same):
        return jnp.where(same, 1.0, 0.0).astype(F32)

    for load in loads:
        load.wait()

    coupled = [one_if(groups[r] == groups[2 * c + q]) for q in range(2)]
    turned = []
    for q in range(2):
        t = jnp.transpose(fcols[q])[:16] * coupled[q]
        srow[0, 8 * q : 8 * q + 8, :] = t[:8]
        srow[1, 8 * q : 8 * q + 8, :] = t[8:]
        turned.append(t[:, :128])
    own_maps = [tile_map[4 * r + t] for t in range(4)]
    other_maps = [tile_map[4 * other + t] for t in range(4)]
    heads = []
    for target in (r, other):
        total = jnp.zeros((16, TS), F32)
        for t in range(4):
            total = total + child[:, t * TS : (t + 1) * TS].astype(F32) * one_if(own_maps[t] == 4 * target)
        heads.append(total)

    def second8(x):
        return pltpu.roll(x, 120, axis=1)

    tall = jnp.concatenate(
        [
            turned[0][:8], turned[1][:8], turned[0][8:], turned[1][8:],
            second8(turned[0])[8:], second8(turned[1])[8:], jnp.zeros((16, 128), F32),
            heads[0], heads[1], second8(heads[0]), second8(heads[1]),
        ],
        axis=0,
    )
    zin[...] = jnp.transpose(tall)[:8]

    pl.semaphore_wait(barrier, chips + cols - 1 + jnp.where(t_self, 0, 1))

    def z_copy(i):
        return pltpu.make_async_remote_copy(
            src_ref=zin, dst_ref=zbuf.at[core, z], send_sem=z_s.at[i], recv_sem=z_r.at[i],
            device_id=(lax.rem(r + 2 * i + 2, rows), c), device_id_type=MESH)

    def share_copy():
        return pltpu.make_async_remote_copy(
            src_ref=zbuf.at[core], dst_ref=zbuf.at[core],
            send_sem=z_s.at[chips - 1], recv_sem=z_r.at[chips - 1],
            device_id=(2 * z + 1 - core, c), device_id_type=MESH)

    def partner_copy():
        return pltpu.make_async_remote_copy(
            src_ref=child, dst_ref=partner, send_sem=p_s, recv_sem=p_r,
            device_id=(other, c), device_id_type=MESH)

    loop(chips - 1, lambda i: z_copy(i).start())
    partner_copy().start()
    zbuf[core, pl.ds(z, 1)] = zin[...][None]

    own8 = pl.ds(pl.multiple_of(r * 8, 8), 8)
    own16 = pl.ds(pl.multiple_of(c * 16, 16), 16)
    for k in range(2):
        for q in range(2):
            strip_c[k, own8, q * MT : (q + 1) * MT] = (
                frows[8 * k : 8 * k + 8, q * MT : (q + 1) * MT] * coupled[q])
    strip_r[:, own16, :] = srow[...]

    def slot(shift):
        return lax.rem(z + shift + chips, chips) * 2 + core

    def piece(a, row):
        if a == 0:
            return strip_c.at[:, pl.ds(pl.multiple_of(row * 8, 8), 8), :]
        return v_c.at[row]

    def ring_copy(a, way, s):
        sign = 1 - 2 * way
        ref = piece(a, slot(-sign * s))
        return pltpu.make_async_remote_copy(
            src_ref=ref, dst_ref=ref, send_sem=ring_s.at[a, way, s], recv_sem=ring_r.at[a, way, s],
            device_id=(slot(sign), c), device_id_type=MESH)

    def sib_copy(a, row):
        ref = piece(a, row)
        return pltpu.make_async_remote_copy(
            src_ref=ref, dst_ref=ref, send_sem=sib_s.at[a, row // 2], recv_sem=sib_r.at[a, row // 2],
            device_id=(2 * z + 1 - core, c), device_id_type=MESH)

    hops = chips // 2

    def ring_start(a, s):
        ring_copy(a, 0, s).start()

        @pl.when(s < hops - 1)
        def _():
            ring_copy(a, 1, s).start()

        sib_copy(a, slot(-s)).start()

        @pl.when(s > 0)
        def _():
            sib_copy(a, slot(s)).start()

    def ring_wait(a, s):
        ring_copy(a, 0, s).wait_recv()

        @pl.when(s < hops - 1)
        def _():
            ring_copy(a, 1, s).wait_recv()

    def ring_next(a, s):
        ring_wait(a, s)

        @pl.when(s < hops - 1)
        def _():
            ring_start(a, s + 1)

        @pl.when(s == hops - 1)
        def _():
            sib_copy(a, slot(hops)).start()

    ring_start(0, 0)

    listed = jnp.transpose(jnp.broadcast_to(map_lanes[...].astype(F32), (128, 128)))
    count = map_lanes.shape[1]
    at_lane = lax.broadcasted_iota(jnp.int32, (128, 128), 1).astype(F32)
    child_id = lax.broadcasted_iota(jnp.int32, (128, 128), 0)
    hits = jnp.where(jnp.logical_and(listed == at_lane, child_id >= count // 2), 1.0, 0.0)
    second = jnp.broadcast_to(jnp.sum(hits, axis=0, keepdims=True), (8, 128)).astype(BF16)

    def spread(tile_of_lane, lanes):
        tile = lax.broadcasted_iota(jnp.int32, (128, lanes), 0)
        lane = lax.broadcasted_iota(jnp.int32, (128, lanes), 1)
        chosen = jnp.where(tile == tile_of_lane(lane), 1.0, 0.0).astype(BF16)
        return dot1(second, chosen, 1, 0).astype(BF16)

    flag_p = spread(lambda lane: 4 * lax.shift_right_logical(lane, 3), PW)[0:1]
    flags[0:8, :height] = spread(lambda lane: 4 * r + lax.shift_right_logical(lane, 7), height).astype(F32)
    flags[0:8, height:] = spread(lambda lane: 8 * c + lax.shift_right_logical(lane, 7), width).astype(F32)

    def plane_copy(a, src, dst, i):
        return pltpu.make_async_remote_copy(
            src_ref=src, dst_ref=dst, send_sem=plane_s.at[a, i], recv_sem=plane_r.at[a, i],
            device_id=(r, lax.rem(c + i + 1, cols)), device_id_type=MESH)

    def sr_copy(i):
        return plane_copy(0, srow, strip_r.at[:, own16, :], i)

    def d_copy(i):
        return plane_copy(1, dpiece.at[0], diag.at[0, own16, :], i)

    def d1_copy(i):
        return plane_copy(4, dpiece.at[pl.ds(1, 2)], diag.at[pl.ds(1, 2), own16, :], i)

    def vp_copy(i):
        return plane_copy(2, vpiece, vpiv.at[:, own16, :], i)

    def vr_copy(i):
        return plane_copy(3, placed, v_r.at[own16, :], i)

    loop(chips - 1, lambda i: z_copy(i).wait_recv())
    share_copy().start()
    ring_next(0, 0)
    share_copy().wait_recv()
    flat = jnp.transpose(
        jnp.concatenate([zbuf[i % 2, i // 2] for i in range(rows)], axis=0))
    dpiece[0] = flat[0:16]
    dpiece[1] = flat[16:32]
    dpiece[2] = flat[32:48]
    half = rows * 4

    def swapped_halves(x):
        return jnp.concatenate([x[:, half:], x[:, :half]], axis=1)

    vpiece[0] = (flat[64:80] + swapped_halves(flat[80:96])).astype(BF16)
    vpiece[1] = (flat[96:112] + swapped_halves(flat[112:128])).astype(BF16)
    diag[:, own16, :] = dpiece[...]
    vpiv[:, own16, :] = vpiece[...]
    loop(cols - 1, lambda i: vp_copy(i).start())
    loop(cols - 1, lambda i: d_copy(i).start())
    loop(cols - 1, lambda i: d1_copy(i).start())

    partner_copy().wait_recv()
    for j in range(height // TS):
        total = jnp.zeros((16, TS), F32)
        for t in range(4):
            at = slice(t * TS, (t + 1) * TS)
            total = total + child[:, at].astype(F32) * one_if(own_maps[t] == 4 * r + j)
            total = total + partner[:, at].astype(F32) * one_if(other_maps[t] == 4 * r + j)
        placed[:, j * TS : (j + 1) * TS] = total.astype(BF16)
    v_r[own16, :] = placed[...]

    def t_copy():
        return pltpu.make_async_remote_copy(
            src_ref=placed, dst_ref=v_c.at[t_row], send_sem=t_s, recv_sem=t_r,
            device_id=(t_row, t_col), device_id_type=MESH)

    @pl.when(t_self)
    def _():
        v_c[pl.ds(r, 1)] = placed[...][None]

    @pl.when(jnp.logical_not(t_self))
    def _():
        t_copy().start()

    loop(cols - 1, lambda i: vr_copy(i).start())
    loop(cols - 1, lambda i: sr_copy(i).start())

    ring_next(0, 1)

    @pl.when(jnp.logical_not(t_self))
    def _():
        t_copy().wait_recv()

    ring_start(1, 0)

    def ring_beside(first):
        def beside(b):
            t = first + b // 2

            @pl.when(jnp.logical_and(b % 2 == 1, t < hops - 2))
            def _():
                ring_next(0, t + 2)

            @pl.when(jnp.logical_and(b % 2 == 0, t > 0))
            def _():
                ring_next(1, t - 1)

        return beside

    loop(cols - 1, lambda i: vp_copy(i).wait_recv())
    for k in range(2):
        vp = vpiv[k]
        wp[k, PW:, :] = vp * flag_p
        wp[k, :PW, :] = vp - vp * flag_p
    i = lax.broadcasted_iota(jnp.int32, (PW, PW), 0)
    j = lax.broadcasted_iota(jnp.int32, (PW, PW), 1)
    eye = jnp.where(i == j, 1.0, 0.0).astype(F32)
    outer = dot1(wp[0], wp[0], 0, 0)
    loop(cols - 1, lambda i: d_copy(i).wait_recv())
    work[:, :PW] = diag[0] + outer
    work[:, PW:] = eye
    factor(work, ring_beside(0))
    x0[...] = left3(work[:, PW:])
    loop(cols - 1, lambda i: d1_copy(i).wait_recv())
    low = diag[1] + dot1(wp[1], wp[0], 0, 0)
    p01[...] = dot1(right3(low, 1), x0[...], 1, 1).astype(BF16)

    work[:, :PW] = diag[2] + dot1(wp[1], wp[1], 0, 0) - dot1(p01[...], p01[...], 1, 1)
    work[:, PW:] = eye
    factor(work, ring_beside(hops // 2))
    x1[...] = left3(work[:, PW:])
    ring_next(1, hops - 1)

    for copy in (sr_copy, vr_copy):
        loop(cols - 1, lambda i: copy(i).wait_recv())

    def tile(strip, v, flag, out, at, sign):
        flag = flag.astype(BF16)
        bottom = v * flag
        top = v - bottom
        out[0:PW, at] = top
        out[PW : 2 * PW, at] = bottom
        w = jnp.concatenate([top, bottom], axis=0)
        s0 = strip[0, :, at] + dot1(wp[0], w, 0, 0)
        first = dot1(x0[...], right3(s0, 0), 1, 0).astype(BF16)
        out[2 * PW : 3 * PW, at] = first * sign
        s1 = strip[1, :, at] + dot1(wp[1], w, 0, 0) - dot1(p01[...], first, 1, 0)
        second = dot1(x1[...], right3(s1, 0), 1, 0).astype(BF16)
        out[3 * PW : 4 * PW, at] = second * sign

    for h in range(height // PW):
        at = slice(h * PW, (h + 1) * PW)
        tile(strip_r, v_r[:, at], flags[0:1, at], out_a, at, BF16(1))
    for a in range(2):
        loop(chips, lambda i: sib_copy(a, 2 * i + core).wait_recv())
    for q in range(2):
        for h in range(height // PW):
            sub = slice(h * PW, (h + 1) * PW)
            at = slice(q * height + h * PW, q * height + (h + 1) * PW)
            v = jnp.concatenate([v_c[2 * i + q, :, sub] for i in range(chips)], axis=0)
            lanes = slice(height + at.start, height + at.stop)
            tile(strip_c, v, flags[0:1, lanes], out_b, at, BF16(-1))

    loop(chips - 1, lambda i: z_copy(i).wait_send())
    share_copy().wait_send()
    partner_copy().wait_send()

    @pl.when(jnp.logical_not(t_self))
    def _():
        t_copy().wait_send()

    for copy in (sr_copy, d_copy, d1_copy, vp_copy, vr_copy):
        loop(cols - 1, lambda i: copy(i).wait_send())
    for a in range(2):
        loop(chips, lambda i: sib_copy(a, 2 * i + core).wait_send())
        loop(hops, lambda s: ring_copy(a, 0, s).wait_send())
        loop(hops - 1, lambda s: ring_copy(a, 1, s).wait_send())


def panels(front, child, tile_group, row_map, rows, cols):
    vmem = pl.BlockSpec(memory_space=pltpu.VMEM)
    dma = pltpu.SemaphoreType.DMA
    shape = jax.ShapeDtypeStruct
    height, width = front.shape
    return pl.pallas_call(
        front_kernel,
        out_shape=(shape((4 * PW, height), BF16), shape((4 * PW, width), BF16)),
        in_specs=[pl.BlockSpec(memory_space=pltpu.HBM)] * 5,
        out_specs=(vmem, vmem),
        scratch_shapes=[
            pltpu.VMEM((2, height, 128), F32),
            pltpu.VMEM((16, width), F32),
            pltpu.VMEM((16, height), BF16),
            pltpu.SMEM(tile_group.shape, jnp.int32),
            pltpu.SMEM(row_map.shape, jnp.int32),
            pltpu.VMEM((1, row_map.shape[0]), jnp.int32),
            dma((7,)),
            pltpu.VMEM((8, 128), F32),
            pltpu.VMEM((2, 16, height), F32),
            pltpu.VMEM((2, rows // 2, 8, 128), F32),
            pltpu.VMEM((16, height), BF16),
            pltpu.VMEM((16, height), BF16),
            pltpu.VMEM((3, 16, PW), F32),
            pltpu.VMEM((2, 16, PW), BF16),
            pltpu.VMEM((3, PW, PW), F32),
            pltpu.VMEM((2, PW, PW), BF16),
            pltpu.VMEM((2, PW, height), F32),
            pltpu.VMEM((2, PW, width), F32),
            pltpu.VMEM((PW, height), BF16),
            pltpu.VMEM((rows, 16, height), BF16),
            pltpu.VMEM((8, height + width), F32),
            pltpu.VMEM((PW, 2 * PW), F32),
            pltpu.VMEM((2, 2 * PW, PW), BF16),
            pltpu.VMEM((PW, 3 * PW), BF16),
            pltpu.VMEM((PW, 3 * PW), BF16),
            pltpu.VMEM((PW, PW), BF16),
            dma((rows // 2,)), dma((rows // 2,)), dma, dma, dma, dma,
            dma((5, cols - 1)), dma((5, cols - 1)),
            dma((2, 2, rows // 4)), dma((2, 2, rows // 4)),
            dma((2, rows // 2)), dma((2, rows // 2)),
        ],
        compiler_params=pltpu.CompilerParams(
            collective_id=0, has_side_effects=True, vmem_limit_bytes=40 << 20),
    )(*(
        pltpu.with_memory_space_constraint(x, pltpu.HBM)
        for x in (front, child, tile_group, row_map, row_map.reshape(1, -1))))


def final_kernel(front, left, right, groups, schur_hbm, panel, done, sem):
    r = lax.axis_index("row")
    c = lax.axis_index("col")
    rows, width = front.shape
    wide = done.shape[2]
    ii = lax.broadcasted_iota(jnp.int32, (rows, wide), 0)
    jj = lax.broadcasted_iota(jnp.int32, (rows, wide), 1)
    copies = []
    for g in range(width // wide):
        at = slice(g * wide, (g + 1) * wide)
        keep = jnp.logical_and(ii >= 16, lax.rem(jj + g * wide, MT) >= 16)
        coupled = jnp.where(groups[r] == groups[2 * c + (g * wide) // MT], 1.0, 0.0).astype(F32)
        total = front[:, at] * coupled + dot1(left[...], right[:, at], 0, 0)
        done[g] = jnp.where(keep, total, 0.0)
        copies.append(pltpu.make_async_copy(done.at[g], schur_hbm.at[:, pl.ds(g * wide, wide)], sem.at[g]))
        copies[-1].start()
    at = pl.multiple_of(c * 16, 16)
    m = lax.broadcasted_iota(jnp.int32, (16, rows), 0) + c * 16
    a = lax.broadcasted_iota(jnp.int32, (16, rows), 1)
    p0 = left[pl.ds(2 * PW + at, 16), :].astype(F32)
    p1 = left[pl.ds(3 * PW + at, 16), :].astype(F32)
    p0 = jnp.where(jnp.logical_or(a >= 8, m <= r * 8 + a), p0, 0.0)
    p1 = jnp.where(jnp.logical_or(a >= 16, m <= r * 8 + a - 8), p1, 0.0)
    p1 = jnp.where(a >= 8, p1, 0.0)
    panel[0:16, :] = p0.astype(BF16)
    panel[16:32, :] = p1.astype(BF16)
    for copy in copies:
        copy.wait()


def final(front, left, right, tile_group):
    rows, width = front.shape
    step = 256
    vmem = pl.BlockSpec(memory_space=pltpu.VMEM)
    return pl.pallas_call(
        final_kernel,
        out_shape=(
            jax.ShapeDtypeStruct((rows, width), F32),
            jax.ShapeDtypeStruct((32, rows), BF16),
        ),
        in_specs=[vmem, vmem, vmem, pl.BlockSpec(memory_space=pltpu.SMEM)],
        out_specs=(pl.BlockSpec(memory_space=pltpu.HBM), vmem),
        scratch_shapes=[
            pltpu.VMEM((width // step, rows, step), F32),
            pltpu.SemaphoreType.DMA((width // step,)),
        ],
        compiler_params=pltpu.CompilerParams(vmem_limit_bytes=16 << 20),
    )(front, left, right, tile_group)


def local(front, tile_group, child, row_map):
    rows = lax.axis_size("row")
    cols = lax.axis_size("col")
    left, right = panels(front, child.T, tile_group, row_map, rows, cols)
    schur, panel = final(front, left, right, tile_group)
    return panel.T, schur


def solution(mesh):
    placed = (P("row", "col"), P(), P("row", "col"), P())
    return jax.shard_map(
        local,
        mesh=mesh,
        in_specs=placed,
        out_specs=(P("row", "col"), P("row", "col")),
        check_vma=False,
    )
```

```python
import functools

import jax
import jax.numpy as jnp
from jax import lax
from jax.experimental import pallas as pl
from jax.experimental.pallas import tpu as pltpu
from jax.sharding import PartitionSpec as P

PW = 256
NP = 2
TS = 128
MT = 512
NB = 64
F32 = jnp.float32
BF16 = jnp.bfloat16
MESH = pl.DeviceIdType.MESH


def loop(count, body):
    def step(i, carry):
        body(i)
        return carry

    lax.fori_loop(0, count, step, 0)


def split3(x):
    high = x.astype(BF16)
    rest = x - high.astype(F32)
    mid = rest.astype(BF16)
    return high, mid, (rest - mid.astype(F32)).astype(BF16)


def dot6(a, b, ca, cb):
    ah, am, al = split3(a)
    bh, bm, bl = split3(b)
    left = jnp.concatenate([ah, ah, am, ah, al, am], axis=ca)
    right = jnp.concatenate([bh, bm, bh, bl, bh, bm], axis=cb)
    return lax.dot_general(left, right, (((ca,), (cb,)), ((), ())), preferred_element_type=F32)


def dot1(a, b, ca, cb):
    return lax.dot_general(a, b, (((ca,), (cb,)), ((), ())), preferred_element_type=F32)


def block_inverse(block):
    ii = lax.broadcasted_iota(jnp.int32, (8, 128), 0)
    ll = lax.broadcasted_iota(jnp.int32, (8, 128), 1)
    groups = NB // 8
    m = []
    for g in range(groups):
        unit = jnp.where(ll == ii + (8 * g + NB), 1.0, 0.0).astype(F32)
        m.append(jnp.where(ll < NB, block[8 * g : 8 * g + 8, :], unit))
    for g in range(groups):
        low = 8 * g
        rest = range(g + 1, groups)
        rows = [jnp.broadcast_to(m[g][i : i + 1, :], (8, 128)) for i in range(8)]
        s = {}
        for i in range(8):
            for k in range(i, 8):
                s[i, k] = jnp.broadcast_to(rows[i][:, low + k : low + k + 1], (8, 128))
        cols = {}
        for h in rest:
            for k in range(8):
                cols[h, k] = jnp.broadcast_to(m[h][:, low + k : low + k + 1], (8, 128))
        for j in range(8):
            inv = lax.rsqrt(s[j, j])
            for k in range(j + 1, 8):
                s[j, k] = s[j, k] * inv
            for i in range(j + 1, 8):
                for k in range(i, 8):
                    s[i, k] = s[i, k] - s[j, i] * s[j, k]
            rows[j] = rows[j] * inv
            for i in range(j + 1, 8):
                rows[i] = rows[i] - s[j, i] * rows[j]
            for h in rest:
                cols[h, j] = cols[h, j] * inv
                for i in range(j + 1, 8):
                    cols[h, i] = cols[h, i] - s[j, i] * cols[h, j]
        merged = rows[0]
        for i in range(1, 8):
            merged = jnp.where(ii == i, rows[i], merged)
        m[g] = merged
        for h in rest:
            for j in range(8):
                m[h] = m[h] - cols[h, j] * rows[j]
    return jnp.concatenate(m, axis=0)[:, NB : 2 * NB]


def factor_step(work, b, beside, extra):
    lane = lax.broadcasted_iota(jnp.int32, (NB, PW), 1)
    beside(2 * b)
    here = pl.ds(pl.multiple_of(b * NB, NB), NB)
    band = work[here, :]
    lead = pltpu.roll(band[:, :PW], (PW - b * NB) % PW, axis=1)
    inverse = block_inverse(lead[:, :128])
    beside(2 * b + 1)
    extra(b)
    upper = dot6(inverse, band, 1, 0)
    below = jnp.where(lane >= (b + 1) * NB, upper[:, :PW], 0.0)
    work[...] -= dot6(below, upper, 0, 0)
    work[here, :] = upper


def split2(x, axis):
    high = x.astype(BF16)
    low = (x - high.astype(F32)).astype(BF16)
    return high, low


def left3(x):
    high, low = split2(x, 1)
    return jnp.concatenate([high, high, low], axis=1)


def right3(x, axis):
    high, low = split2(x, axis)
    return jnp.concatenate([high, low, high], axis=axis)


def front_kernel(
    front_hbm, child_hbm, groups_hbm, map_hbm, lanes_hbm,
    out_a, out_b, own_p,
    fcols, frows, child, groups, tile_map, map_lanes, in_s,
    zin, srow, zbuf, partner, placed, dpiece, vpiece,
    diag, vpiv, strip_r, strip_c, v_r, v_c, flags,
    work, wp, x0, x1, p01, turned_r, later,
    z_s, z_r, p_s, p_r, t_s, t_r,
    plane_s, plane_r, ring_s, ring_r, sib_s, sib_r, d_s, d_r,
):
    r = lax.axis_index("row")
    c = lax.axis_index("col")
    rows = lax.axis_size("row")
    cols = lax.axis_size("col")
    height, width = front_hbm.shape
    z = r // 2
    core = r % 2
    chips = rows // 2
    other = lax.rem(r + chips, rows)
    t_row = 2 * c + core
    t_col = z
    t_self = jnp.logical_and(t_row == r, t_col == c)

    barrier = pltpu.get_barrier_semaphore()

    loads = [
        pltpu.make_async_copy(src, dst, in_s.at[i])
        for i, (src, dst) in enumerate([
            (front_hbm.at[:, pl.ds(0, 128)], fcols.at[0]),
            (front_hbm.at[:, pl.ds(MT, 128)], fcols.at[1]),
            (child_hbm, child),
            (groups_hbm, groups),
            (map_hbm, tile_map),
            (front_hbm.at[pl.ds(0, 16), :], frows),
            (lanes_hbm, map_lanes),
        ])
    ]
    for load in loads:
        load.start()

    def hello(row, col):
        pl.semaphore_signal(barrier, inc=1, device_id=(row, col), device_id_type=MESH)

    loop(chips - 1, lambda i: hello(lax.rem(r + 2 * i + 2, rows), c))
    loop(cols - 1, lambda i: hello(r, lax.rem(c + i + 1, cols)))
    hello(2 * z + 1 - core, c)

    @pl.when(jnp.logical_not(t_self))
    def _():
        pl.semaphore_signal(barrier, inc=1, device_id=(t_row, t_col), device_id_type=MESH)

    def one_if(same):
        return jnp.where(same, 1.0, 0.0).astype(F32)

    for load in loads:
        load.wait()

    coupled = [one_if(groups[r] == groups[2 * c + q]) for q in range(2)]
    turned = []
    for q in range(2):
        t = jnp.transpose(fcols[q])[:16] * coupled[q]
        srow[0, 8 * q : 8 * q + 8, :] = t[:8]
        srow[1, 8 * q : 8 * q + 8, :] = t[8:]
        turned.append(t[:, :128])
    own_maps = [tile_map[4 * r + t] for t in range(4)]
    other_maps = [tile_map[4 * other + t] for t in range(4)]
    heads = []
    for target in (r, other):
        total = jnp.zeros((16, TS), F32)
        for t in range(4):
            total = total + child[:, t * TS : (t + 1) * TS].astype(F32) * one_if(own_maps[t] == 4 * target)
        heads.append(total)

    def second8(x):
        return pltpu.roll(x, 120, axis=1)

    tall = jnp.concatenate(
        [
            turned[0][:8], turned[1][:8], turned[0][8:], turned[1][8:],
            second8(turned[0])[8:], second8(turned[1])[8:], jnp.zeros((16, 128), F32),
            heads[0], heads[1], second8(heads[0]), second8(heads[1]),
        ],
        axis=0,
    )
    zin[...] = jnp.transpose(tall)[:8]

    pl.semaphore_wait(barrier, chips + cols - 1 + jnp.where(t_self, 0, 1))

    def z_copy(i):
        return pltpu.make_async_remote_copy(
            src_ref=zin, dst_ref=zbuf.at[core, z], send_sem=z_s.at[i], recv_sem=z_r.at[i],
            device_id=(lax.rem(r + 2 * i + 2, rows), c), device_id_type=MESH)

    def share_copy():
        return pltpu.make_async_remote_copy(
            src_ref=zbuf.at[core], dst_ref=zbuf.at[core],
            send_sem=z_s.at[chips - 1], recv_sem=z_r.at[chips - 1],
            device_id=(2 * z + 1 - core, c), device_id_type=MESH)

    def partner_copy():
        return pltpu.make_async_remote_copy(
            src_ref=child, dst_ref=partner, send_sem=p_s, recv_sem=p_r,
            device_id=(other, c), device_id_type=MESH)

    loop(chips - 1, lambda i: z_copy(i).start())
    partner_copy().start()
    zbuf[core, pl.ds(z, 1)] = zin[...][None]

    own8 = pl.ds(pl.multiple_of(r * 8, 8), 8)
    own16 = pl.ds(pl.multiple_of(c * 16, 16), 16)
    for k in range(2):
        for q in range(2):
            strip_c[k, own8, q * MT : (q + 1) * MT] = (
                frows[8 * k : 8 * k + 8, q * MT : (q + 1) * MT] * coupled[q])
    strip_r[:, own16, :] = srow[...]

    def slot(shift):
        return lax.rem(z + shift + chips, chips) * 2 + core

    def piece(a, row):
        if a == 0:
            return strip_c.at[:, pl.ds(pl.multiple_of(row * 8, 8), 8), :]
        return v_c.at[row]

    def ring_copy(a, way, s):
        sign = 1 - 2 * way
        ref = piece(a, slot(-sign * s))
        return pltpu.make_async_remote_copy(
            src_ref=ref, dst_ref=ref, send_sem=ring_s.at[a, way, s], recv_sem=ring_r.at[a, way, s],
            device_id=(slot(sign), c), device_id_type=MESH)

    def sib_copy(a, row):
        ref = piece(a, row)
        return pltpu.make_async_remote_copy(
            src_ref=ref, dst_ref=ref, send_sem=sib_s.at[a, row // 2], recv_sem=sib_r.at[a, row // 2],
            device_id=(2 * z + 1 - core, c), device_id_type=MESH)

    hops = chips // 2

    def ring_start(a, s):
        ring_copy(a, 0, s).start()

        @pl.when(s < hops - 1)
        def _():
            ring_copy(a, 1, s).start()

        sib_copy(a, slot(-s)).start()

        @pl.when(s > 0)
        def _():
            sib_copy(a, slot(s)).start()

    def ring_wait(a, s):
        ring_copy(a, 0, s).wait_recv()

        @pl.when(s < hops - 1)
        def _():
            ring_copy(a, 1, s).wait_recv()

    def ring_next(a, s):
        ring_wait(a, s)

        @pl.when(s < hops - 1)
        def _():
            ring_start(a, s + 1)

        @pl.when(s == hops - 1)
        def _():
            sib_copy(a, slot(hops)).start()

    ring_start(0, 0)

    def plane_copy(a, src, dst, i):
        return pltpu.make_async_remote_copy(
            src_ref=src, dst_ref=dst, send_sem=plane_s.at[a, i], recv_sem=plane_r.at[a, i],
            device_id=(r, lax.rem(c + i + 1, cols)), device_id_type=MESH)

    def sr_copy(i):
        return plane_copy(0, srow, strip_r.at[:, own16, :], i)

    def d_copy(i):
        return plane_copy(1, dpiece.at[0], diag.at[0, own16, :], i)

    def d1_copy(i):
        return plane_copy(4, dpiece.at[1 + core], diag.at[1 + core, own16, :], i)

    def d1_share():
        return pltpu.make_async_remote_copy(
            src_ref=diag.at[1 + core], dst_ref=diag.at[1 + core], send_sem=d_s, recv_sem=d_r,
            device_id=(2 * z + 1 - core, c), device_id_type=MESH)

    def vp_copy(i):
        return plane_copy(2, vpiece, vpiv.at[:, own16, :], i)

    def vr_copy(i):
        return plane_copy(3, placed, v_r.at[own16, :], i)

    ring_next(0, 0)

    partner_copy().wait_recv()
    for j in range(height // TS):
        total = jnp.zeros((16, TS), F32)
        for t in range(4):
            at = slice(t * TS, (t + 1) * TS)
            total = total + child[:, at].astype(F32) * one_if(own_maps[t] == 4 * r + j)
            total = total + partner[:, at].astype(F32) * one_if(other_maps[t] == 4 * r + j)
        placed[:, j * TS : (j + 1) * TS] = total.astype(BF16)
    v_r[own16, :] = placed[...]

    def t_copy():
        return pltpu.make_async_remote_copy(
            src_ref=placed, dst_ref=v_c.at[t_row], send_sem=t_s, recv_sem=t_r,
            device_id=(t_row, t_col), device_id_type=MESH)

    @pl.when(t_self)
    def _():
        v_c[pl.ds(r, 1)] = placed[...][None]

    @pl.when(jnp.logical_not(t_self))
    def _():
        t_copy().start()

    loop(chips - 1, lambda i: z_copy(i).wait_recv())
    share_copy().start()
    ring_next(0, 1)
    share_copy().wait_recv()
    flat = jnp.transpose(
        jnp.concatenate([zbuf[i % 2, i // 2] for i in range(rows)], axis=0))
    dpiece[0] = flat[0:16]
    dpiece[1] = flat[16:32]
    dpiece[2] = flat[32:48]
    half = rows * 4

    def swapped_halves(x):
        return jnp.concatenate([x[:, half:], x[:, :half]], axis=1)

    vpiece[0] = (flat[64:80] + swapped_halves(flat[80:96])).astype(BF16)
    vpiece[1] = (flat[96:112] + swapped_halves(flat[112:128])).astype(BF16)
    diag[0, own16, :] = dpiece[0]
    diag[1 + core, own16, :] = dpiece[1 + core]
    vpiv[:, own16, :] = vpiece[...]
    loop(cols - 1, lambda i: vp_copy(i).start())
    loop(cols - 1, lambda i: d_copy(i).start())
    loop(cols - 1, lambda i: d1_copy(i).start())

    loop(cols - 1, lambda i: vr_copy(i).start())
    loop(cols - 1, lambda i: sr_copy(i).start())

    @pl.when(jnp.logical_not(t_self))
    def _():
        t_copy().wait_recv()

    ring_start(1, 0)
    ring_next(0, 2)

    listed = jnp.transpose(jnp.broadcast_to(map_lanes[...].astype(F32), (128, 128)))
    count = map_lanes.shape[1]
    at_lane = lax.broadcasted_iota(jnp.int32, (128, 128), 1).astype(F32)
    child_id = lax.broadcasted_iota(jnp.int32, (128, 128), 0)
    hits = jnp.where(jnp.logical_and(listed == at_lane, child_id >= count // 2), 1.0, 0.0)
    second = jnp.broadcast_to(jnp.sum(hits, axis=0, keepdims=True), (8, 128)).astype(BF16)

    def spread(tile_of_lane, lanes):
        tile = lax.broadcasted_iota(jnp.int32, (128, lanes), 0)
        lane = lax.broadcasted_iota(jnp.int32, (128, lanes), 1)
        chosen = jnp.where(tile == tile_of_lane(lane), 1.0, 0.0).astype(BF16)
        return dot1(second, chosen, 1, 0).astype(BF16)

    flag_p = spread(lambda lane: 4 * lax.shift_right_logical(lane, 3), PW)[0:1]
    flags[0:8, :height] = spread(lambda lane: 4 * r + lax.shift_right_logical(lane, 7), height).astype(F32)
    flags[0:8, height:] = spread(lambda lane: 8 * c + lax.shift_right_logical(lane, 7), width).astype(F32)

    ring_next(0, 3)
    ring_next(1, 0)

    loop(cols - 1, lambda i: vp_copy(i).wait_recv())
    for k in range(2):
        vp = vpiv[k]
        wp[k, PW:, :] = vp * flag_p
        wp[k, :PW, :] = vp - vp * flag_p
    i = lax.broadcasted_iota(jnp.int32, (PW, PW), 0)
    j = lax.broadcasted_iota(jnp.int32, (PW, PW), 1)
    eye = jnp.where(i == j, 1.0, 0.0).astype(F32)
    work[:, :PW] = dot1(wp[0], wp[0], 0, 0)
    work[:, PW:] = eye
    ring_next(0, 4)
    ring_next(1, 1)
    loop(cols - 1, lambda i: d_copy(i).wait_recv())
    work[:, :PW] += diag[0]

    def beside(t):
        @pl.when(t == 1)
        def _():
            ring_next(0, 5)
            ring_next(1, 2)

        @pl.when(t == 3)
        def _():
            ring_next(0, 6)
            ring_next(1, 3)

        @pl.when(t == 5)
        def _():
            ring_next(0, 7)
            ring_next(1, 4)
            loop(cols - 1, lambda i: d1_copy(i).wait_recv())
            d1_share().start()

        @pl.when(t == 7)
        def _():
            ring_next(1, 5)

    loop(PW // NB, lambda b: factor_step(work, b, beside, lambda b: None))
    x0[...] = left3(work[:, PW:])
    d1_share().wait_recv()
    ring_next(1, 6)
    low = diag[1] + dot1(wp[1], wp[0], 0, 0)
    p01[...] = dot1(right3(low, 1), x0[...], 1, 1).astype(BF16)

    work[:, :PW] = diag[2] + dot1(wp[1], wp[1], 0, 0) - dot1(p01[...], p01[...], 1, 1)
    work[:, PW:] = eye

    def first_part(strip, v, flag, at):
        flag = flag.astype(BF16)
        bottom = v * flag
        w = jnp.concatenate([v - bottom, bottom], axis=0)
        s0 = strip[0, :, at] + dot1(wp[0], w, 0, 0)
        first = dot1(x0[...], right3(s0, 0), 1, 0).astype(BF16)
        s1 = strip[1, :, at] + dot1(wp[1], w, 0, 0) - dot1(p01[...], first, 1, 0)
        return w, first, right3(s1, 0)

    def col_tile(q, h):
        sub = slice(h * PW, (h + 1) * PW)
        at = slice(q * height + h * PW, q * height + (h + 1) * PW)
        v = jnp.concatenate([v_c[2 * i + q, :, sub] for i in range(chips)], axis=0)
        flag = flags[0:1, height + at.start : height + at.stop]
        w, first, rest = first_part(strip_c, v, flag, at)
        out_b[0 : 2 * PW, at] = w
        out_b[2 * PW : 3 * PW, at] = -first
        later[:, at] = rest

    tiles = [(q, h) for q in range(2) for h in range(height // PW)]

    def beside_second(t):
        if t == 2:
            ring_next(1, 7)
            for a in range(2):
                loop(chips, lambda i: sib_copy(a, 2 * i + core).wait_recv())

    def extra_second(b):
        if b == 2:
            col_tile(*tiles[0])
            col_tile(*tiles[1])
        if b == 3:
            col_tile(*tiles[2])
            col_tile(*tiles[3])

    for b in range(PW // NB):
        factor_step(work, b, beside_second, extra_second)
    x1[...] = left3(work[:, PW:])

    for q, h in tiles:
        at = slice(q * height + h * PW, q * height + (h + 1) * PW)
        out_b[3 * PW : 4 * PW, at] = -dot1(x1[...], later[:, at], 1, 0).astype(BF16)

    for copy in (sr_copy, vr_copy):
        loop(cols - 1, lambda i: copy(i).wait_recv())
    for h in range(height // PW):
        at = slice(h * PW, (h + 1) * PW)
        w, first, rest = first_part(strip_r, v_r[:, at], flags[0:1, at], at)
        second = dot1(x1[...], rest, 1, 0).astype(BF16)
        turned_r[0:PW, at] = first
        turned_r[PW:, at] = second
        out_a[at, 0 : 2 * PW] = jnp.transpose(w)
        out_a[at, 2 * PW : 3 * PW] = jnp.transpose(first)
        out_a[at, 3 * PW : 4 * PW] = jnp.transpose(second)
    own_p[0:16, :] = turned_r[own16, :]
    own_p[16:32, :] = turned_r[pl.ds(pl.multiple_of(PW + c * 16, 16), 16), :]

    loop(chips - 1, lambda i: z_copy(i).wait_send())
    share_copy().wait_send()
    d1_share().wait_send()
    partner_copy().wait_send()

    @pl.when(jnp.logical_not(t_self))
    def _():
        t_copy().wait_send()

    for copy in (sr_copy, d_copy, d1_copy, vp_copy, vr_copy):
        loop(cols - 1, lambda i: copy(i).wait_send())
    for a in range(2):
        loop(chips, lambda i: sib_copy(a, 2 * i + core).wait_send())
        loop(hops, lambda s: ring_copy(a, 0, s).wait_send())
        loop(hops - 1, lambda s: ring_copy(a, 1, s).wait_send())


def panels(front, child, tile_group, row_map, rows, cols):
    vmem = pl.BlockSpec(memory_space=pltpu.VMEM)
    dma = pltpu.SemaphoreType.DMA
    shape = jax.ShapeDtypeStruct
    height, width = front.shape
    return pl.pallas_call(
        front_kernel,
        out_shape=(
            shape((height, 4 * PW), BF16), shape((4 * PW, width), BF16), shape((32, height), BF16)),
        in_specs=[pl.BlockSpec(memory_space=pltpu.HBM)] * 5,
        out_specs=(vmem, vmem, vmem),
        scratch_shapes=[
            pltpu.VMEM((2, height, 128), F32),
            pltpu.VMEM((16, width), F32),
            pltpu.VMEM((16, height), BF16),
            pltpu.SMEM(tile_group.shape, jnp.int32),
            pltpu.SMEM(row_map.shape, jnp.int32),
            pltpu.VMEM((1, row_map.shape[0]), jnp.int32),
            dma((7,)),
            pltpu.VMEM((8, 128), F32),
            pltpu.VMEM((2, 16, height), F32),
            pltpu.VMEM((2, rows // 2, 8, 128), F32),
            pltpu.VMEM((16, height), BF16),
            pltpu.VMEM((16, height), BF16),
            pltpu.VMEM((3, 16, PW), F32),
            pltpu.VMEM((2, 16, PW), BF16),
            pltpu.VMEM((3, PW, PW), F32),
            pltpu.VMEM((2, PW, PW), BF16),
            pltpu.VMEM((2, PW, height), F32),
            pltpu.VMEM((2, PW, width), F32),
            pltpu.VMEM((PW, height), BF16),
            pltpu.VMEM((rows, 16, height), BF16),
            pltpu.VMEM((8, height + width), F32),
            pltpu.VMEM((PW, 2 * PW), F32),
            pltpu.VMEM((2, 2 * PW, PW), BF16),
            pltpu.VMEM((PW, 3 * PW), BF16),
            pltpu.VMEM((PW, 3 * PW), BF16),
            pltpu.VMEM((PW, PW), BF16),
            pltpu.VMEM((2 * PW, height), BF16),
            pltpu.VMEM((3 * PW, width), BF16),
            dma((rows // 2,)), dma((rows // 2,)), dma, dma, dma, dma,
            dma((5, cols - 1)), dma((5, cols - 1)),
            dma((2, 2, rows // 4)), dma((2, 2, rows // 4)),
            dma((2, rows // 2)), dma((2, rows // 2)), dma, dma,
        ],
        compiler_params=pltpu.CompilerParams(
            collective_id=0, has_side_effects=True, vmem_limit_bytes=40 << 20),
    )(*(
        pltpu.with_memory_space_constraint(x, pltpu.HBM)
        for x in (front, child, tile_group, row_map, row_map.reshape(1, -1))))


def final_kernel(front, left, right, own_p, groups, schur_hbm, panel, done, sem):
    r = lax.axis_index("row")
    c = lax.axis_index("col")
    rows, width = front.shape
    wide = done.shape[2]
    ii = lax.broadcasted_iota(jnp.int32, (rows, wide), 0)
    jj = lax.broadcasted_iota(jnp.int32, (rows, wide), 1)
    copies = []
    for g in range(width // wide):
        at = slice(g * wide, (g + 1) * wide)
        keep = jnp.logical_and(ii >= 16, lax.rem(jj + g * wide, MT) >= 16)
        coupled = jnp.where(groups[r] == groups[2 * c + (g * wide) // MT], 1.0, 0.0).astype(F32)
        total = front[:, at] * coupled + dot1(left[...], right[:, at], 1, 0)
        done[g] = jnp.where(keep, total, 0.0)
        copies.append(pltpu.make_async_copy(done.at[g], schur_hbm.at[:, pl.ds(g * wide, wide)], sem.at[g]))
        copies[-1].start()
    m = lax.broadcasted_iota(jnp.int32, (16, rows), 0) + c * 16
    a = lax.broadcasted_iota(jnp.int32, (16, rows), 1)
    p0 = own_p[0:16, :].astype(F32)
    p1 = own_p[16:32, :].astype(F32)
    p0 = jnp.where(jnp.logical_or(a >= 8, m <= r * 8 + a), p0, 0.0)
    p1 = jnp.where(jnp.logical_or(a >= 16, m <= r * 8 + a - 8), p1, 0.0)
    p1 = jnp.where(a >= 8, p1, 0.0)
    panel[0:16, :] = p0.astype(BF16)
    panel[16:32, :] = p1.astype(BF16)
    for copy in copies:
        copy.wait()


def final(front, left, right, own_p, tile_group):
    rows, width = front.shape
    step = 256
    vmem = pl.BlockSpec(memory_space=pltpu.VMEM)
    return pl.pallas_call(
        final_kernel,
        out_shape=(
            jax.ShapeDtypeStruct((rows, width), F32),
            jax.ShapeDtypeStruct((32, rows), BF16),
        ),
        in_specs=[vmem, vmem, vmem, vmem, pl.BlockSpec(memory_space=pltpu.SMEM)],
        out_specs=(pl.BlockSpec(memory_space=pltpu.HBM), vmem),
        scratch_shapes=[
            pltpu.VMEM((width // step, rows, step), F32),
            pltpu.SemaphoreType.DMA((width // step,)),
        ],
        compiler_params=pltpu.CompilerParams(vmem_limit_bytes=16 << 20),
    )(front, left, right, own_p, tile_group)


def local(front, tile_group, child, row_map):
    rows = lax.axis_size("row")
    cols = lax.axis_size("col")
    left, right, own_p = panels(front, child.T, tile_group, row_map, rows, cols)
    schur, panel = final(front, left, right, own_p, tile_group)
    return panel.T, schur


def solution(mesh):
    placed = (P("row", "col"), P(), P("row", "col"), P())
    return jax.shard_map(
        local,
        mesh=mesh,
        in_specs=placed,
        out_specs=(P("row", "col"), P("row", "col")),
        check_vma=False,
    )
```

```python
import functools

import jax
import jax.numpy as jnp
from jax import lax
from jax.experimental import pallas as pl
from jax.experimental.pallas import tpu as pltpu
from jax.sharding import PartitionSpec as P

PW = 256
NP = 2
TS = 128
MT = 512
NB = 64
F32 = jnp.float32
BF16 = jnp.bfloat16
MESH = pl.DeviceIdType.MESH


def loop(count, body):
    def step(i, carry):
        body(i)
        return carry

    lax.fori_loop(0, count, step, 0)


def split3(x):
    high = x.astype(BF16)
    rest = x - high.astype(F32)
    mid = rest.astype(BF16)
    return high, mid, (rest - mid.astype(F32)).astype(BF16)


def dot6(a, b, ca, cb):
    ah, am, al = split3(a)
    bh, bm, bl = split3(b)
    left = jnp.concatenate([ah, ah, am, ah, al, am], axis=ca)
    right = jnp.concatenate([bh, bm, bh, bl, bh, bm], axis=cb)
    return lax.dot_general(left, right, (((ca,), (cb,)), ((), ())), preferred_element_type=F32)


def dot1(a, b, ca, cb):
    return lax.dot_general(a, b, (((ca,), (cb,)), ((), ())), preferred_element_type=F32)


def block_inverse(block):
    ii = lax.broadcasted_iota(jnp.int32, (8, 128), 0)
    ll = lax.broadcasted_iota(jnp.int32, (8, 128), 1)
    groups = NB // 8
    m = []
    for g in range(groups):
        unit = jnp.where(ll == ii + (8 * g + NB), 1.0, 0.0).astype(F32)
        m.append(jnp.where(ll < NB, block[8 * g : 8 * g + 8, :], unit))
    for g in range(groups):
        low = 8 * g
        rest = range(g + 1, groups)
        rows = [jnp.broadcast_to(m[g][i : i + 1, :], (8, 128)) for i in range(8)]
        s = {}
        for i in range(8):
            for k in range(i, 8):
                s[i, k] = jnp.broadcast_to(rows[i][:, low + k : low + k + 1], (8, 128))
        cols = {}
        for h in rest:
            for k in range(8):
                cols[h, k] = jnp.broadcast_to(m[h][:, low + k : low + k + 1], (8, 128))
        for j in range(8):
            inv = lax.rsqrt(s[j, j])
            for k in range(j + 1, 8):
                s[j, k] = s[j, k] * inv
            for i in range(j + 1, 8):
                for k in range(i, 8):
                    s[i, k] = s[i, k] - s[j, i] * s[j, k]
            rows[j] = rows[j] * inv
            for i in range(j + 1, 8):
                rows[i] = rows[i] - s[j, i] * rows[j]
            for h in rest:
                cols[h, j] = cols[h, j] * inv
                for i in range(j + 1, 8):
                    cols[h, i] = cols[h, i] - s[j, i] * cols[h, j]
        merged = rows[0]
        for i in range(1, 8):
            merged = jnp.where(ii == i, rows[i], merged)
        m[g] = merged
        for h in rest:
            for j in range(8):
                m[h] = m[h] - cols[h, j] * rows[j]
    return jnp.concatenate(m, axis=0)[:, NB : 2 * NB]


def factor_step(work, b, beside, extra):
    lane = lax.broadcasted_iota(jnp.int32, (NB, PW), 1)
    beside(2 * b)
    here = pl.ds(pl.multiple_of(b * NB, NB), NB)
    band = work[here, :]
    lead = pltpu.roll(band[:, :PW], (PW - b * NB) % PW, axis=1)
    inverse = block_inverse(lead[:, :128])
    beside(2 * b + 1)
    extra(b)
    upper = dot6(inverse, band, 1, 0)
    below = jnp.where(lane >= (b + 1) * NB, upper[:, :PW], 0.0)
    work[...] -= dot6(below, upper, 0, 0)
    work[here, :] = upper


def split2(x, axis):
    high = x.astype(BF16)
    low = (x - high.astype(F32)).astype(BF16)
    return high, low


def left3(x):
    high, low = split2(x, 1)
    return jnp.concatenate([high, high, low], axis=1)


def right3(x, axis):
    high, low = split2(x, axis)
    return jnp.concatenate([high, low, high], axis=axis)


def front_kernel(
    front_hbm, child_hbm, groups_hbm, map_hbm, lanes_hbm,
    out_a, out_b, own_p,
    fcols, frows, child, groups, tile_map, map_lanes, in_s,
    zin, srow, zbuf, partner, placed, dpiece, vpiece,
    diag, vpiv, strip_r, strip_c, v_r, v_c, flags,
    work, wp, x0, x1, p01, turned_r, later,
    z_s, z_r, p_s, p_r, t_s, t_r,
    plane_s, plane_r, ring_s, ring_r, sib_s, sib_r, d_s, d_r,
):
    r = lax.axis_index("row")
    c = lax.axis_index("col")
    rows = lax.axis_size("row")
    cols = lax.axis_size("col")
    height, width = front_hbm.shape
    z = r // 2
    core = r % 2
    chips = rows // 2
    other = lax.rem(r + chips, rows)
    t_row = 2 * c + core
    t_col = z
    t_self = jnp.logical_and(t_row == r, t_col == c)

    barrier = pltpu.get_barrier_semaphore()

    loads = [
        pltpu.make_async_copy(src, dst, in_s.at[i])
        for i, (src, dst) in enumerate([
            (front_hbm.at[:, pl.ds(0, 128)], fcols.at[0]),
            (front_hbm.at[:, pl.ds(MT, 128)], fcols.at[1]),
            (child_hbm, child),
            (groups_hbm, groups),
            (map_hbm, tile_map),
            (front_hbm.at[pl.ds(0, 16), :], frows),
            (lanes_hbm, map_lanes),
        ])
    ]
    for load in loads:
        load.start()

    def hello(row, col):
        pl.semaphore_signal(barrier, inc=1, device_id=(row, col), device_id_type=MESH)

    loop(chips - 1, lambda i: hello(lax.rem(r + 2 * i + 2, rows), c))
    loop(cols - 1, lambda i: hello(r, lax.rem(c + i + 1, cols)))
    hello(2 * z + 1 - core, c)

    @pl.when(jnp.logical_not(t_self))
    def _():
        pl.semaphore_signal(barrier, inc=1, device_id=(t_row, t_col), device_id_type=MESH)

    def one_if(same):
        return jnp.where(same, 1.0, 0.0).astype(F32)

    for load in loads:
        load.wait()

    coupled = [one_if(groups[r] == groups[2 * c + q]) for q in range(2)]
    turned = []
    for q in range(2):
        t = jnp.transpose(fcols[q])[:16] * coupled[q]
        srow[0, 8 * q : 8 * q + 8, :] = t[:8]
        srow[1, 8 * q : 8 * q + 8, :] = t[8:]
        turned.append(t[:, :128])
    own_maps = [tile_map[4 * r + t] for t in range(4)]
    other_maps = [tile_map[4 * other + t] for t in range(4)]
    heads = []
    for target in (r, other):
        total = jnp.zeros((16, TS), F32)
        for t in range(4):
            total = total + child[:, t * TS : (t + 1) * TS].astype(F32) * one_if(own_maps[t] == 4 * target)
        heads.append(total)

    def second8(x):
        return pltpu.roll(x, 120, axis=1)

    tall = jnp.concatenate(
        [
            turned[0][:8], turned[1][:8], turned[0][8:], turned[1][8:],
            second8(turned[0])[8:], second8(turned[1])[8:], jnp.zeros((16, 128), F32),
            heads[0], heads[1], second8(heads[0]), second8(heads[1]),
        ],
        axis=0,
    )
    zin[...] = jnp.transpose(tall)[:8]

    pl.semaphore_wait(barrier, chips + cols - 1 + jnp.where(t_self, 0, 1))

    def z_copy(i):
        return pltpu.make_async_remote_copy(
            src_ref=zin, dst_ref=zbuf.at[core, z], send_sem=z_s.at[i], recv_sem=z_r.at[i],
            device_id=(lax.rem(r + 2 * i + 2, rows), c), device_id_type=MESH)

    def share_copy():
        return pltpu.make_async_remote_copy(
            src_ref=zbuf.at[core], dst_ref=zbuf.at[core],
            send_sem=z_s.at[chips - 1], recv_sem=z_r.at[chips - 1],
            device_id=(2 * z + 1 - core, c), device_id_type=MESH)

    def partner_copy():
        return pltpu.make_async_remote_copy(
            src_ref=child, dst_ref=partner, send_sem=p_s, recv_sem=p_r,
            device_id=(other, c), device_id_type=MESH)

    loop(chips - 1, lambda i: z_copy(i).start())
    partner_copy().start()
    zbuf[core, pl.ds(z, 1)] = zin[...][None]

    own16 = pl.ds(pl.multiple_of(c * 16, 16), 16)
    for q in range(2):
        at = slice(q * MT, (q + 1) * MT)
        strip_c[pl.ds(r, 1), :, at] = (frows[:, at] * coupled[q]).astype(BF16)[None]
    strip_r[:, own16, :] = srow[...]

    def slot(shift):
        return lax.rem(z + shift + chips, chips) * 2 + core

    def piece(a, row):
        return strip_c.at[row] if a == 0 else v_c.at[row]

    def ring_copy(a, way, distance):
        sign = 1 - 2 * way
        near = distance <= 2
        ref = piece(a, slot(0) if near else slot(-sign * (distance - 2)))
        return pltpu.make_async_remote_copy(
            src_ref=ref, dst_ref=ref,
            send_sem=ring_s.at[a, way, distance - 1], recv_sem=ring_r.at[a, way, distance - 1],
            device_id=(slot(sign * (distance if near else 2)), c), device_id_type=MESH)

    def sib_copy(a, row):
        ref = piece(a, row)
        return pltpu.make_async_remote_copy(
            src_ref=ref, dst_ref=ref, send_sem=sib_s.at[a, row // 2], recv_sem=sib_r.at[a, row // 2],
            device_id=(2 * z + 1 - core, c), device_id_type=MESH)

    hops = chips // 2

    def ring_pairs(stage):
        return [(way, d) for d in (2 * stage + 1, 2 * stage + 2) for way in range(2) if d < hops or way == 0]

    def ring_next(a, stage):
        if stage == 0:
            sib_copy(a, slot(0)).start()
        else:
            for way, d in ring_pairs(stage - 1):
                ring_copy(a, way, d).wait_recv()
        if stage < hops // 2:
            for way, d in ring_pairs(stage):
                ring_copy(a, way, d).start()
        if stage > 0:
            for way, d in ring_pairs(stage - 1):
                sib_copy(a, slot(-(1 - 2 * way) * d)).start()

    ring_next(0, 0)

    def plane_copy(a, src, dst, i):
        return pltpu.make_async_remote_copy(
            src_ref=src, dst_ref=dst, send_sem=plane_s.at[a, i], recv_sem=plane_r.at[a, i],
            device_id=(r, lax.rem(c + i + 1, cols)), device_id_type=MESH)

    def sr_copy(i):
        return plane_copy(0, srow, strip_r.at[:, own16, :], i)

    def d_copy(i):
        return plane_copy(1, dpiece.at[0], diag.at[0, own16, :], i)

    def d1_copy(i):
        return plane_copy(4, dpiece.at[1 + core], diag.at[1 + core, own16, :], i)

    def d1_share():
        return pltpu.make_async_remote_copy(
            src_ref=diag.at[1 + core], dst_ref=diag.at[1 + core], send_sem=d_s, recv_sem=d_r,
            device_id=(2 * z + 1 - core, c), device_id_type=MESH)

    def vp_copy(i):
        return plane_copy(2, vpiece, vpiv.at[:, own16, :], i)

    def vr_copy(i):
        return plane_copy(3, placed, v_r.at[own16, :], i)

    partner_copy().wait_recv()
    for j in range(height // TS):
        total = jnp.zeros((16, TS), F32)
        for t in range(4):
            at = slice(t * TS, (t + 1) * TS)
            total = total + child[:, at].astype(F32) * one_if(own_maps[t] == 4 * r + j)
            total = total + partner[:, at].astype(F32) * one_if(other_maps[t] == 4 * r + j)
        placed[:, j * TS : (j + 1) * TS] = total.astype(BF16)
    v_r[own16, :] = placed[...]

    def t_copy():
        return pltpu.make_async_remote_copy(
            src_ref=placed, dst_ref=v_c.at[t_row], send_sem=t_s, recv_sem=t_r,
            device_id=(t_row, t_col), device_id_type=MESH)

    @pl.when(t_self)
    def _():
        v_c[pl.ds(r, 1)] = placed[...][None]

    @pl.when(jnp.logical_not(t_self))
    def _():
        t_copy().start()

    ring_next(0, 1)

    loop(chips - 1, lambda i: z_copy(i).wait_recv())
    share_copy().start()
    share_copy().wait_recv()
    flat = jnp.transpose(
        jnp.concatenate([zbuf[i % 2, i // 2] for i in range(rows)], axis=0))
    dpiece[0] = flat[0:16]
    dpiece[1] = flat[16:32]
    dpiece[2] = flat[32:48]
    half = rows * 4

    def swapped_halves(x):
        return jnp.concatenate([x[:, half:], x[:, :half]], axis=1)

    vpiece[0] = (flat[64:80] + swapped_halves(flat[80:96])).astype(BF16)
    vpiece[1] = (flat[96:112] + swapped_halves(flat[112:128])).astype(BF16)
    diag[0, own16, :] = dpiece[0]
    diag[1 + core, own16, :] = dpiece[1 + core]
    vpiv[:, own16, :] = vpiece[...]
    loop(cols - 1, lambda i: vp_copy(i).start())
    loop(cols - 1, lambda i: d_copy(i).start())
    loop(cols - 1, lambda i: d1_copy(i).start())

    loop(cols - 1, lambda i: vr_copy(i).start())
    loop(cols - 1, lambda i: sr_copy(i).start())

    @pl.when(jnp.logical_not(t_self))
    def _():
        t_copy().wait_recv()

    ring_next(1, 0)
    ring_next(0, 2)

    listed = jnp.transpose(jnp.broadcast_to(map_lanes[...].astype(F32), (128, 128)))
    count = map_lanes.shape[1]
    at_lane = lax.broadcasted_iota(jnp.int32, (128, 128), 1).astype(F32)
    child_id = lax.broadcasted_iota(jnp.int32, (128, 128), 0)
    hits = jnp.where(jnp.logical_and(listed == at_lane, child_id >= count // 2), 1.0, 0.0)
    second = jnp.broadcast_to(jnp.sum(hits, axis=0, keepdims=True), (8, 128)).astype(BF16)

    def spread(tile_of_lane, lanes):
        tile = lax.broadcasted_iota(jnp.int32, (128, lanes), 0)
        lane = lax.broadcasted_iota(jnp.int32, (128, lanes), 1)
        chosen = jnp.where(tile == tile_of_lane(lane), 1.0, 0.0).astype(BF16)
        return dot1(second, chosen, 1, 0).astype(BF16)

    flag_p = spread(lambda lane: 4 * lax.shift_right_logical(lane, 3), PW)[0:1]
    flags[0:8, :height] = spread(lambda lane: 4 * r + lax.shift_right_logical(lane, 7), height).astype(F32)
    flags[0:8, height:] = spread(lambda lane: 8 * c + lax.shift_right_logical(lane, 7), width).astype(F32)

    loop(cols - 1, lambda i: vp_copy(i).wait_recv())
    for k in range(2):
        vp = vpiv[k]
        wp[k, PW:, :] = vp * flag_p
        wp[k, :PW, :] = vp - vp * flag_p
    i = lax.broadcasted_iota(jnp.int32, (PW, PW), 0)
    j = lax.broadcasted_iota(jnp.int32, (PW, PW), 1)
    eye = jnp.where(i == j, 1.0, 0.0).astype(F32)
    work[:, :PW] = dot1(wp[0], wp[0], 0, 0)
    work[:, PW:] = eye
    ring_next(0, 3)
    ring_next(1, 1)
    loop(cols - 1, lambda i: d_copy(i).wait_recv())
    work[:, :PW] += diag[0]

    def beside(t):
        if t == 2:
            ring_next(1, 2)
        if t == 3:
            ring_next(0, 4)
        if t == 5:
            ring_next(1, 3)
            loop(cols - 1, lambda i: d1_copy(i).wait_recv())
            d1_share().start()

    for b in range(PW // NB):
        factor_step(work, b, beside, lambda b: None)
    x0[...] = left3(work[:, PW:])
    d1_share().wait_recv()
    ring_next(1, 4)
    low = diag[1] + dot1(wp[1], wp[0], 0, 0)
    p01[...] = dot1(right3(low, 1), x0[...], 1, 1).astype(BF16)

    work[:, :PW] = diag[2] + dot1(wp[1], wp[1], 0, 0) - dot1(p01[...], p01[...], 1, 1)
    work[:, PW:] = eye

    def first_part(strip0, strip1, v, flag):
        flag = flag.astype(BF16)
        bottom = v * flag
        w = jnp.concatenate([v - bottom, bottom], axis=0)
        s0 = strip0 + dot1(wp[0], w, 0, 0)
        first = dot1(x0[...], right3(s0, 0), 1, 0).astype(BF16)
        s1 = strip1 + dot1(wp[1], w, 0, 0) - dot1(p01[...], first, 1, 0)
        return w, first, right3(s1, 0)

    def col_tile(q, h):
        sub = slice(h * PW, (h + 1) * PW)
        at = slice(q * height + h * PW, q * height + (h + 1) * PW)
        v = jnp.concatenate([v_c[2 * i + q, :, sub] for i in range(chips)], axis=0)
        flag = flags[0:1, height + at.start : height + at.stop]
        strip = strip_c[:, :, at].astype(F32)
        w, first, rest = first_part(
            strip[:, :8].reshape(PW, PW), strip[:, 8:].reshape(PW, PW), v, flag)
        out_b[0 : 2 * PW, at] = w
        out_b[2 * PW : 3 * PW, at] = -first
        later[:, at] = rest

    tiles = [(q, h) for q in range(2) for h in range(height // PW)]

    def beside_second(t):
        if t == 2:
            for a in range(2):
                loop(chips, lambda i: sib_copy(a, 2 * i + core).wait_recv())

    def extra_second(b):
        if b == 2:
            col_tile(*tiles[0])
            col_tile(*tiles[1])
        if b == 3:
            col_tile(*tiles[2])
            col_tile(*tiles[3])

    for b in range(PW // NB):
        factor_step(work, b, beside_second, extra_second)
    x1[...] = left3(work[:, PW:])

    for q, h in tiles:
        at = slice(q * height + h * PW, q * height + (h + 1) * PW)
        out_b[3 * PW : 4 * PW, at] = -dot1(x1[...], later[:, at], 1, 0).astype(BF16)

    for copy in (sr_copy, vr_copy):
        loop(cols - 1, lambda i: copy(i).wait_recv())
    for h in range(height // PW):
        at = slice(h * PW, (h + 1) * PW)
        w, first, rest = first_part(
            strip_r[0, :, at], strip_r[1, :, at], v_r[:, at], flags[0:1, at])
        second = dot1(x1[...], rest, 1, 0).astype(BF16)
        turned_r[0:PW, at] = first
        turned_r[PW:, at] = second
        out_a[at, 0 : 2 * PW] = jnp.transpose(w)
        out_a[at, 2 * PW : 3 * PW] = jnp.transpose(first)
        out_a[at, 3 * PW : 4 * PW] = jnp.transpose(second)
    own_p[0:16, :] = turned_r[own16, :]
    own_p[16:32, :] = turned_r[pl.ds(pl.multiple_of(PW + c * 16, 16), 16), :]

    loop(chips - 1, lambda i: z_copy(i).wait_send())
    share_copy().wait_send()
    d1_share().wait_send()
    partner_copy().wait_send()

    @pl.when(jnp.logical_not(t_self))
    def _():
        t_copy().wait_send()

    for copy in (sr_copy, d_copy, d1_copy, vp_copy, vr_copy):
        loop(cols - 1, lambda i: copy(i).wait_send())
    for a in range(2):
        loop(chips, lambda i: sib_copy(a, 2 * i + core).wait_send())
        for stage in range(hops // 2):
            for way, d in ring_pairs(stage):
                ring_copy(a, way, d).wait_send()


def panels(front, child, tile_group, row_map, rows, cols):
    vmem = pl.BlockSpec(memory_space=pltpu.VMEM)
    dma = pltpu.SemaphoreType.DMA
    shape = jax.ShapeDtypeStruct
    height, width = front.shape
    return pl.pallas_call(
        front_kernel,
        out_shape=(
            shape((height, 4 * PW), BF16), shape((4 * PW, width), BF16), shape((32, height), BF16)),
        in_specs=[pl.BlockSpec(memory_space=pltpu.HBM)] * 5,
        out_specs=(vmem, vmem, vmem),
        scratch_shapes=[
            pltpu.VMEM((2, height, 128), F32),
            pltpu.VMEM((16, width), F32),
            pltpu.VMEM((16, height), BF16),
            pltpu.SMEM(tile_group.shape, jnp.int32),
            pltpu.SMEM(row_map.shape, jnp.int32),
            pltpu.VMEM((1, row_map.shape[0]), jnp.int32),
            dma((7,)),
            pltpu.VMEM((8, 128), F32),
            pltpu.VMEM((2, 16, height), F32),
            pltpu.VMEM((2, rows // 2, 8, 128), F32),
            pltpu.VMEM((16, height), BF16),
            pltpu.VMEM((16, height), BF16),
            pltpu.VMEM((3, 16, PW), F32),
            pltpu.VMEM((2, 16, PW), BF16),
            pltpu.VMEM((3, PW, PW), F32),
            pltpu.VMEM((2, PW, PW), BF16),
            pltpu.VMEM((2, PW, height), F32),
            pltpu.VMEM((rows, 16, width), BF16),
            pltpu.VMEM((PW, height), BF16),
            pltpu.VMEM((rows, 16, height), BF16),
            pltpu.VMEM((8, height + width), F32),
            pltpu.VMEM((PW, 2 * PW), F32),
            pltpu.VMEM((2, 2 * PW, PW), BF16),
            pltpu.VMEM((PW, 3 * PW), BF16),
            pltpu.VMEM((PW, 3 * PW), BF16),
            pltpu.VMEM((PW, PW), BF16),
            pltpu.VMEM((2 * PW, height), BF16),
            pltpu.VMEM((3 * PW, width), BF16),
            dma((rows // 2,)), dma((rows // 2,)), dma, dma, dma, dma,
            dma((5, cols - 1)), dma((5, cols - 1)),
            dma((2, 2, rows // 4)), dma((2, 2, rows // 4)),
            dma((2, rows // 2)), dma((2, rows // 2)), dma, dma,
        ],
        compiler_params=pltpu.CompilerParams(
            collective_id=0, has_side_effects=True, vmem_limit_bytes=40 << 20),
    )(*(
        pltpu.with_memory_space_constraint(x, pltpu.HBM)
        for x in (front, child, tile_group, row_map, row_map.reshape(1, -1))))


def final_kernel(front, left, right, own_p, groups, schur_hbm, panel, done, sem):
    r = lax.axis_index("row")
    c = lax.axis_index("col")
    rows, width = front.shape
    wide = done.shape[2]
    ii = lax.broadcasted_iota(jnp.int32, (rows, wide), 0)
    jj = lax.broadcasted_iota(jnp.int32, (rows, wide), 1)
    copies = []
    for g in range(width // wide):
        at = slice(g * wide, (g + 1) * wide)
        keep = jnp.logical_and(ii >= 16, lax.rem(jj + g * wide, MT) >= 16)
        coupled = jnp.where(groups[r] == groups[2 * c + (g * wide) // MT], 1.0, 0.0).astype(F32)
        total = front[:, at] * coupled + dot1(left[...], right[:, at], 1, 0)
        done[g] = jnp.where(keep, total, 0.0)
        copies.append(pltpu.make_async_copy(done.at[g], schur_hbm.at[:, pl.ds(g * wide, wide)], sem.at[g]))
        copies[-1].start()
    m = lax.broadcasted_iota(jnp.int32, (16, rows), 0) + c * 16
    a = lax.broadcasted_iota(jnp.int32, (16, rows), 1)
    p0 = own_p[0:16, :].astype(F32)
    p1 = own_p[16:32, :].astype(F32)
    p0 = jnp.where(jnp.logical_or(a >= 8, m <= r * 8 + a), p0, 0.0)
    p1 = jnp.where(jnp.logical_or(a >= 16, m <= r * 8 + a - 8), p1, 0.0)
    p1 = jnp.where(a >= 8, p1, 0.0)
    panel[0:16, :] = p0.astype(BF16)
    panel[16:32, :] = p1.astype(BF16)
    for copy in copies:
        copy.wait()


def final(front, left, right, own_p, tile_group):
    rows, width = front.shape
    step = 256
    vmem = pl.BlockSpec(memory_space=pltpu.VMEM)
    return pl.pallas_call(
        final_kernel,
        out_shape=(
            jax.ShapeDtypeStruct((rows, width), F32),
            jax.ShapeDtypeStruct((32, rows), BF16),
        ),
        in_specs=[vmem, vmem, vmem, vmem, pl.BlockSpec(memory_space=pltpu.SMEM)],
        out_specs=(pl.BlockSpec(memory_space=pltpu.HBM), vmem),
        scratch_shapes=[
            pltpu.VMEM((width // step, rows, step), F32),
            pltpu.SemaphoreType.DMA((width // step,)),
        ],
        compiler_params=pltpu.CompilerParams(vmem_limit_bytes=16 << 20),
    )(front, left, right, own_p, tile_group)


def local(front, tile_group, child, row_map):
    rows = lax.axis_size("row")
    cols = lax.axis_size("col")
    left, right, own_p = panels(front, child.T, tile_group, row_map, rows, cols)
    schur, panel = final(front, left, right, own_p, tile_group)
    return panel.T, schur


def solution(mesh):
    placed = (P("row", "col"), P(), P("row", "col"), P())
    return jax.shard_map(
        local,
        mesh=mesh,
        in_specs=placed,
        out_specs=(P("row", "col"), P("row", "col")),
        check_vma=False,
    )
```

```python
import functools

import jax
import jax.numpy as jnp
from jax import lax
from jax.experimental import pallas as pl
from jax.experimental.pallas import tpu as pltpu
from jax.sharding import PartitionSpec as P

PW = 256
NP = 2
TS = 128
MT = 512
NB = 64
F32 = jnp.float32
BF16 = jnp.bfloat16
MESH = pl.DeviceIdType.MESH


def loop(count, body):
    def step(i, carry):
        body(i)
        return carry

    lax.fori_loop(0, count, step, 0)


def split3(x):
    high = x.astype(BF16)
    rest = x - high.astype(F32)
    mid = rest.astype(BF16)
    return high, mid, (rest - mid.astype(F32)).astype(BF16)


def dot6(a, b, ca, cb):
    ah, am, al = split3(a)
    bh, bm, bl = split3(b)
    left = jnp.concatenate([ah, ah, am, ah, al, am], axis=ca)
    right = jnp.concatenate([bh, bm, bh, bl, bh, bm], axis=cb)
    return lax.dot_general(left, right, (((ca,), (cb,)), ((), ())), preferred_element_type=F32)


def dot1(a, b, ca, cb):
    return lax.dot_general(a, b, (((ca,), (cb,)), ((), ())), preferred_element_type=F32)


def block_inverse(block):
    ii = lax.broadcasted_iota(jnp.int32, (8, 128), 0)
    ll = lax.broadcasted_iota(jnp.int32, (8, 128), 1)
    groups = NB // 8
    m = []
    for g in range(groups):
        unit = jnp.where(ll == ii + (8 * g + NB), 1.0, 0.0).astype(F32)
        m.append(jnp.where(ll < NB, block[8 * g : 8 * g + 8, :], unit))
    for g in range(groups):
        low = 8 * g
        rows = [jnp.broadcast_to(m[g][i : i + 1, :], (8, 128)) for i in range(8)]
        cols = {}
        for h in range(g, groups):
            for k in range(8):
                cols[h, k] = jnp.broadcast_to(m[h][:, low + k : low + k + 1], (8, 128))
        for j in range(8):
            inv = lax.rsqrt(jnp.broadcast_to(cols[g, j][j : j + 1, :], (8, 128)))
            rows[j] = rows[j] * inv
            for h in range(g, groups):
                cols[h, j] = cols[h, j] * inv
            for k in range(j + 1, 8):
                factor = jnp.broadcast_to(cols[g, j][k : k + 1, :], (8, 128))
                for h in range(g, groups):
                    cols[h, k] = cols[h, k] - factor * cols[h, j]
                rows[k] = rows[k] - factor * rows[j]
        merged = rows[0]
        for i in range(1, 8):
            merged = jnp.where(ii == i, rows[i], merged)
        m[g] = merged
        for h in range(g + 1, groups):
            for j in range(8):
                m[h] = m[h] - cols[h, j] * rows[j]
    return jnp.concatenate(m, axis=0)[:, NB : 2 * NB]


def factor_step(work, b, beside, extra):
    lane = lax.broadcasted_iota(jnp.int32, (NB, PW), 1)
    beside(2 * b)
    here = pl.ds(pl.multiple_of(b * NB, NB), NB)
    band = work[here, :]
    lead = pltpu.roll(band[:, :PW], (PW - b * NB) % PW, axis=1)
    inverse = block_inverse(lead[:, :128])
    beside(2 * b + 1)
    extra(b)
    upper = dot6(inverse, band, 1, 0)
    below = jnp.where(lane >= (b + 1) * NB, upper[:, :PW], 0.0)
    work[...] -= dot6(below, upper, 0, 0)
    work[here, :] = upper


def split2(x, axis):
    high = x.astype(BF16)
    low = (x - high.astype(F32)).astype(BF16)
    return high, low


def left3(x):
    high, low = split2(x, 1)
    return jnp.concatenate([high, high, low], axis=1)


def right3(x, axis):
    high, low = split2(x, axis)
    return jnp.concatenate([high, low, high], axis=axis)


def front_kernel(
    front_hbm, child_hbm, groups_hbm, map_hbm, lanes_hbm,
    out_a, out_b, own_p,
    fcols, frows, child, groups, tile_map, map_lanes, in_s,
    zin, srow, zbuf, partner, placed, dpiece, vpiece,
    diag, vpiv, strip_r, strip_c, v_r, v_c, flags,
    work, wp, x0, x1, p01, turned_r, later,
    z_s, z_r, p_s, p_r, t_s, t_r,
    plane_s, plane_r, ring_s, ring_r, sib_s, sib_r, d_s, d_r,
):
    r = lax.axis_index("row")
    c = lax.axis_index("col")
    rows = lax.axis_size("row")
    cols = lax.axis_size("col")
    height, width = front_hbm.shape
    z = r // 2
    core = r % 2
    chips = rows // 2
    other = lax.rem(r + chips, rows)
    t_row = 2 * c + core
    t_col = z
    t_self = jnp.logical_and(t_row == r, t_col == c)

    barrier = pltpu.get_barrier_semaphore()

    loads = [
        pltpu.make_async_copy(src, dst, in_s.at[i])
        for i, (src, dst) in enumerate([
            (front_hbm.at[:, pl.ds(0, 128)], fcols.at[0]),
            (front_hbm.at[:, pl.ds(MT, 128)], fcols.at[1]),
            (child_hbm, child),
            (groups_hbm, groups),
            (map_hbm, tile_map),
            (front_hbm.at[pl.ds(0, 16), :], frows),
            (lanes_hbm, map_lanes),
        ])
    ]
    for load in loads:
        load.start()

    def hello(row, col):
        pl.semaphore_signal(barrier, inc=1, device_id=(row, col), device_id_type=MESH)

    loop(chips - 1, lambda i: hello(lax.rem(r + 2 * i + 2, rows), c))
    loop(cols - 1, lambda i: hello(r, lax.rem(c + i + 1, cols)))
    hello(2 * z + 1 - core, c)

    @pl.when(jnp.logical_not(t_self))
    def _():
        pl.semaphore_signal(barrier, inc=1, device_id=(t_row, t_col), device_id_type=MESH)

    def one_if(same):
        return jnp.where(same, 1.0, 0.0).astype(F32)

    for load in loads:
        load.wait()

    coupled = [one_if(groups[r] == groups[2 * c + q]) for q in range(2)]
    turned = []
    for q in range(2):
        t = jnp.transpose(fcols[q])[:16] * coupled[q]
        srow[0, 8 * q : 8 * q + 8, :] = t[:8]
        srow[1, 8 * q : 8 * q + 8, :] = t[8:]
        turned.append(t[:, :128])
    own_maps = [tile_map[4 * r + t] for t in range(4)]
    other_maps = [tile_map[4 * other + t] for t in range(4)]
    heads = []
    for target in (r, other):
        total = jnp.zeros((16, TS), F32)
        for t in range(4):
            total = total + child[:, t * TS : (t + 1) * TS].astype(F32) * one_if(own_maps[t] == 4 * target)
        heads.append(total)

    def second8(x):
        return pltpu.roll(x, 120, axis=1)

    tall = jnp.concatenate(
        [
            turned[0][:8], turned[1][:8], turned[0][8:], turned[1][8:],
            second8(turned[0])[8:], second8(turned[1])[8:], jnp.zeros((16, 128), F32),
            heads[0], heads[1], second8(heads[0]), second8(heads[1]),
        ],
        axis=0,
    )
    zin[...] = jnp.transpose(tall)[:8]

    pl.semaphore_wait(barrier, chips + cols - 1 + jnp.where(t_self, 0, 1))

    def z_copy(i):
        return pltpu.make_async_remote_copy(
            src_ref=zin, dst_ref=zbuf.at[core, z], send_sem=z_s.at[i], recv_sem=z_r.at[i],
            device_id=(lax.rem(r + 2 * i + 2, rows), c), device_id_type=MESH)

    def share_copy():
        return pltpu.make_async_remote_copy(
            src_ref=zbuf.at[core], dst_ref=zbuf.at[core],
            send_sem=z_s.at[chips - 1], recv_sem=z_r.at[chips - 1],
            device_id=(2 * z + 1 - core, c), device_id_type=MESH)

    def partner_copy():
        return pltpu.make_async_remote_copy(
            src_ref=child, dst_ref=partner, send_sem=p_s, recv_sem=p_r,
            device_id=(other, c), device_id_type=MESH)

    loop(chips - 1, lambda i: z_copy(i).start())
    partner_copy().start()
    zbuf[core, pl.ds(z, 1)] = zin[...][None]

    own16 = pl.ds(pl.multiple_of(c * 16, 16), 16)
    for q in range(2):
        at = slice(q * MT, (q + 1) * MT)
        strip_c[pl.ds(r, 1), :, at] = (frows[:, at] * coupled[q]).astype(BF16)[None]
    strip_r[:, own16, :] = srow[...]

    def slot(shift):
        return lax.rem(z + shift + chips, chips) * 2 + core

    def piece(a, row):
        return strip_c.at[row] if a == 0 else v_c.at[row]

    def ring_copy(a, way, distance):
        sign = 1 - 2 * way
        near = distance <= 2
        ref = piece(a, slot(0) if near else slot(-sign * (distance - 2)))
        return pltpu.make_async_remote_copy(
            src_ref=ref, dst_ref=ref,
            send_sem=ring_s.at[a, way, distance - 1], recv_sem=ring_r.at[a, way, distance - 1],
            device_id=(slot(sign * (distance if near else 2)), c), device_id_type=MESH)

    def sib_copy(a, row):
        ref = piece(a, row)
        return pltpu.make_async_remote_copy(
            src_ref=ref, dst_ref=ref, send_sem=sib_s.at[a, row // 2], recv_sem=sib_r.at[a, row // 2],
            device_id=(2 * z + 1 - core, c), device_id_type=MESH)

    hops = chips // 2

    def ring_pairs(stage):
        return [(way, d) for d in (2 * stage + 1, 2 * stage + 2) for way in range(2) if d < hops or way == 0]

    def ring_next(a, stage):
        if stage == 0:
            sib_copy(a, slot(0)).start()
        else:
            for way, d in ring_pairs(stage - 1):
                ring_copy(a, way, d).wait_recv()
        if stage < hops // 2:
            for way, d in ring_pairs(stage):
                ring_copy(a, way, d).start()
        if stage > 0:
            for way, d in ring_pairs(stage - 1):
                sib_copy(a, slot(-(1 - 2 * way) * d)).start()

    ring_next(0, 0)

    def plane_copy(a, src, dst, i):
        return pltpu.make_async_remote_copy(
            src_ref=src, dst_ref=dst, send_sem=plane_s.at[a, i], recv_sem=plane_r.at[a, i],
            device_id=(r, lax.rem(c + i + 1, cols)), device_id_type=MESH)

    def sr_copy(i):
        return plane_copy(0, srow, strip_r.at[:, own16, :], i)

    def d_copy(i):
        return plane_copy(1, dpiece.at[0], diag.at[0, own16, :], i)

    def d1_copy(i):
        return plane_copy(4, dpiece.at[1 + core], diag.at[1 + core, own16, :], i)

    def d1_share():
        return pltpu.make_async_remote_copy(
            src_ref=diag.at[1 + core], dst_ref=diag.at[1 + core], send_sem=d_s.at[0], recv_sem=d_r.at[0],
            device_id=(2 * z + 1 - core, c), device_id_type=MESH)

    def d_share():
        return pltpu.make_async_remote_copy(
            src_ref=diag.at[0], dst_ref=diag.at[0], send_sem=d_s.at[1], recv_sem=d_r.at[1],
            device_id=(2 * z + 1 - core, c), device_id_type=MESH)

    def vp_share():
        return pltpu.make_async_remote_copy(
            src_ref=vpiv, dst_ref=vpiv, send_sem=d_s.at[2], recv_sem=d_r.at[2],
            device_id=(2 * z + 1 - core, c), device_id_type=MESH)

    def vp_copy(i):
        return plane_copy(2, vpiece, vpiv.at[:, own16, :], i)

    def vr_copy(i):
        return plane_copy(3, placed, v_r.at[own16, :], i)

    partner_copy().wait_recv()
    for j in range(height // TS):
        total = jnp.zeros((16, TS), F32)
        for t in range(4):
            at = slice(t * TS, (t + 1) * TS)
            total = total + child[:, at].astype(F32) * one_if(own_maps[t] == 4 * r + j)
            total = total + partner[:, at].astype(F32) * one_if(other_maps[t] == 4 * r + j)
        placed[:, j * TS : (j + 1) * TS] = total.astype(BF16)
    v_r[own16, :] = placed[...]

    def t_copy():
        return pltpu.make_async_remote_copy(
            src_ref=placed, dst_ref=v_c.at[t_row], send_sem=t_s, recv_sem=t_r,
            device_id=(t_row, t_col), device_id_type=MESH)

    @pl.when(t_self)
    def _():
        v_c[pl.ds(r, 1)] = placed[...][None]

    @pl.when(jnp.logical_not(t_self))
    def _():
        t_copy().start()

    ring_next(0, 1)

    loop(chips - 1, lambda i: z_copy(i).wait_recv())
    share_copy().start()
    share_copy().wait_recv()
    flat = jnp.transpose(
        jnp.concatenate([zbuf[i % 2, i // 2] for i in range(rows)], axis=0))
    dpiece[0] = flat[0:16]
    dpiece[1] = flat[16:32]
    dpiece[2] = flat[32:48]
    half = rows * 4

    def swapped_halves(x):
        return jnp.concatenate([x[:, half:], x[:, :half]], axis=1)

    vpiece[0] = (flat[64:80] + swapped_halves(flat[80:96])).astype(BF16)
    vpiece[1] = (flat[96:112] + swapped_halves(flat[112:128])).astype(BF16)
    diag[1 + core, own16, :] = dpiece[1 + core]

    @pl.when(core == 0)
    def _():
        diag[0, own16, :] = dpiece[0]
        loop(cols - 1, lambda i: d_copy(i).start())

    @pl.when(core == 1)
    def _():
        vpiv[:, own16, :] = vpiece[...]
        loop(cols - 1, lambda i: vp_copy(i).start())

    loop(cols - 1, lambda i: d1_copy(i).start())

    loop(cols - 1, lambda i: vr_copy(i).start())
    loop(cols - 1, lambda i: sr_copy(i).start())

    @pl.when(jnp.logical_not(t_self))
    def _():
        t_copy().wait_recv()

    ring_next(1, 0)
    ring_next(0, 2)

    listed = jnp.transpose(jnp.broadcast_to(map_lanes[...].astype(F32), (128, 128)))
    count = map_lanes.shape[1]
    at_lane = lax.broadcasted_iota(jnp.int32, (128, 128), 1).astype(F32)
    child_id = lax.broadcasted_iota(jnp.int32, (128, 128), 0)
    hits = jnp.where(jnp.logical_and(listed == at_lane, child_id >= count // 2), 1.0, 0.0)
    second = jnp.broadcast_to(jnp.sum(hits, axis=0, keepdims=True), (8, 128)).astype(BF16)

    def spread(tile_of_lane, lanes):
        tile = lax.broadcasted_iota(jnp.int32, (128, lanes), 0)
        lane = lax.broadcasted_iota(jnp.int32, (128, lanes), 1)
        chosen = jnp.where(tile == tile_of_lane(lane), 1.0, 0.0).astype(BF16)
        return dot1(second, chosen, 1, 0).astype(BF16)

    flag_p = spread(lambda lane: 4 * lax.shift_right_logical(lane, 3), PW)[0:1]
    flags[0:8, :height] = spread(lambda lane: 4 * r + lax.shift_right_logical(lane, 7), height).astype(F32)
    flags[0:8, height:] = spread(lambda lane: 8 * c + lax.shift_right_logical(lane, 7), width).astype(F32)

    ring_next(0, 3)
    ring_next(1, 1)

    @pl.when(core == 0)
    def _():
        loop(cols - 1, lambda i: d_copy(i).wait_recv())
        d_share().start()
        vp_share().wait_recv()

    @pl.when(core == 1)
    def _():
        loop(cols - 1, lambda i: vp_copy(i).wait_recv())
        vp_share().start()
        d_share().wait_recv()

    for k in range(2):
        vp = vpiv[k]
        wp[k, PW:, :] = vp * flag_p
        wp[k, :PW, :] = vp - vp * flag_p
    i = lax.broadcasted_iota(jnp.int32, (PW, PW), 0)
    j = lax.broadcasted_iota(jnp.int32, (PW, PW), 1)
    eye = jnp.where(i == j, 1.0, 0.0).astype(F32)
    work[:, :PW] = diag[0] + dot1(wp[0], wp[0], 0, 0)
    work[:, PW:] = eye

    def beside(t):
        if t == 2:
            ring_next(1, 2)
        if t == 3:
            ring_next(0, 4)
        if t == 5:
            ring_next(1, 3)
            loop(cols - 1, lambda i: d1_copy(i).wait_recv())
            d1_share().start()

    for b in range(PW // NB):
        factor_step(work, b, beside, lambda b: None)
    x0[...] = left3(work[:, PW:])
    d1_share().wait_recv()
    ring_next(1, 4)
    low = diag[1] + dot1(wp[1], wp[0], 0, 0)
    p01[...] = dot1(right3(low, 1), x0[...], 1, 1).astype(BF16)

    work[:, :PW] = diag[2] + dot1(wp[1], wp[1], 0, 0) - dot1(p01[...], p01[...], 1, 1)
    work[:, PW:] = eye

    def first_part(strip0, strip1, v, flag):
        flag = flag.astype(BF16)
        bottom = v * flag
        w = jnp.concatenate([v - bottom, bottom], axis=0)
        s0 = strip0 + dot1(wp[0], w, 0, 0)
        first = dot1(x0[...], right3(s0, 0), 1, 0).astype(BF16)
        s1 = strip1 + dot1(wp[1], w, 0, 0) - dot1(p01[...], first, 1, 0)
        return w, first, right3(s1, 0)

    def col_tile(q, h):
        sub = slice(h * PW, (h + 1) * PW)
        at = slice(q * height + h * PW, q * height + (h + 1) * PW)
        v = jnp.concatenate([v_c[2 * i + q, :, sub] for i in range(chips)], axis=0)
        flag = flags[0:1, height + at.start : height + at.stop]
        strip = strip_c[:, :, at].astype(F32)
        w, first, rest = first_part(
            strip[:, :8].reshape(PW, PW), strip[:, 8:].reshape(PW, PW), v, flag)
        out_b[0 : 2 * PW, at] = w
        out_b[2 * PW : 3 * PW, at] = -first
        later[:, at] = rest

    tiles = [(q, h) for q in range(2) for h in range(height // PW)]

    def beside_second(t):
        if t == 2:
            for a in range(2):
                loop(chips, lambda i: sib_copy(a, 2 * i + core).wait_recv())

    def extra_second(b):
        if b == 2:
            col_tile(*tiles[0])
            col_tile(*tiles[1])
        if b == 3:
            col_tile(*tiles[2])
            col_tile(*tiles[3])

    for b in range(PW // NB):
        factor_step(work, b, beside_second, extra_second)
    x1[...] = left3(work[:, PW:])

    for q, h in tiles:
        at = slice(q * height + h * PW, q * height + (h + 1) * PW)
        out_b[3 * PW : 4 * PW, at] = -dot1(x1[...], later[:, at], 1, 0).astype(BF16)

    for copy in (sr_copy, vr_copy):
        loop(cols - 1, lambda i: copy(i).wait_recv())
    for h in range(height // PW):
        at = slice(h * PW, (h + 1) * PW)
        w, first, rest = first_part(
            strip_r[0, :, at], strip_r[1, :, at], v_r[:, at], flags[0:1, at])
        second = dot1(x1[...], rest, 1, 0).astype(BF16)
        turned_r[0:PW, at] = first
        turned_r[PW:, at] = second
        out_a[at, 0 : 2 * PW] = jnp.transpose(w)
        out_a[at, 2 * PW : 3 * PW] = jnp.transpose(first)
        out_a[at, 3 * PW : 4 * PW] = jnp.transpose(second)
    own_p[0:16, :] = turned_r[own16, :]
    own_p[16:32, :] = turned_r[pl.ds(pl.multiple_of(PW + c * 16, 16), 16), :]

    loop(chips - 1, lambda i: z_copy(i).wait_send())
    share_copy().wait_send()
    d1_share().wait_send()
    partner_copy().wait_send()

    @pl.when(jnp.logical_not(t_self))
    def _():
        t_copy().wait_send()

    @pl.when(core == 0)
    def _():
        d_share().wait_send()
        loop(cols - 1, lambda i: d_copy(i).wait_send())

    @pl.when(core == 1)
    def _():
        vp_share().wait_send()
        loop(cols - 1, lambda i: vp_copy(i).wait_send())

    for copy in (sr_copy, d1_copy, vr_copy):
        loop(cols - 1, lambda i: copy(i).wait_send())
    for a in range(2):
        loop(chips, lambda i: sib_copy(a, 2 * i + core).wait_send())
        for stage in range(hops // 2):
            for way, d in ring_pairs(stage):
                ring_copy(a, way, d).wait_send()


def panels(front, child, tile_group, row_map, rows, cols):
    vmem = pl.BlockSpec(memory_space=pltpu.VMEM)
    dma = pltpu.SemaphoreType.DMA
    shape = jax.ShapeDtypeStruct
    height, width = front.shape
    return pl.pallas_call(
        front_kernel,
        out_shape=(
            shape((height, 4 * PW), BF16), shape((4 * PW, width), BF16), shape((32, height), BF16)),
        in_specs=[pl.BlockSpec(memory_space=pltpu.HBM)] * 5,
        out_specs=(vmem, vmem, vmem),
        scratch_shapes=[
            pltpu.VMEM((2, height, 128), F32),
            pltpu.VMEM((16, width), F32),
            pltpu.VMEM((16, height), BF16),
            pltpu.SMEM(tile_group.shape, jnp.int32),
            pltpu.SMEM(row_map.shape, jnp.int32),
            pltpu.VMEM((1, row_map.shape[0]), jnp.int32),
            dma((7,)),
            pltpu.VMEM((8, 128), F32),
            pltpu.VMEM((2, 16, height), F32),
            pltpu.VMEM((2, rows // 2, 8, 128), F32),
            pltpu.VMEM((16, height), BF16),
            pltpu.VMEM((16, height), BF16),
            pltpu.VMEM((3, 16, PW), F32),
            pltpu.VMEM((2, 16, PW), BF16),
            pltpu.VMEM((3, PW, PW), F32),
            pltpu.VMEM((2, PW, PW), BF16),
            pltpu.VMEM((2, PW, height), F32),
            pltpu.VMEM((rows, 16, width), BF16),
            pltpu.VMEM((PW, height), BF16),
            pltpu.VMEM((rows, 16, height), BF16),
            pltpu.VMEM((8, height + width), F32),
            pltpu.VMEM((PW, 2 * PW), F32),
            pltpu.VMEM((2, 2 * PW, PW), BF16),
            pltpu.VMEM((PW, 3 * PW), BF16),
            pltpu.VMEM((PW, 3 * PW), BF16),
            pltpu.VMEM((PW, PW), BF16),
            pltpu.VMEM((2 * PW, height), BF16),
            pltpu.VMEM((3 * PW, width), BF16),
            dma((rows // 2,)), dma((rows // 2,)), dma, dma, dma, dma,
            dma((5, cols - 1)), dma((5, cols - 1)),
            dma((2, 2, rows // 4)), dma((2, 2, rows // 4)),
            dma((2, rows // 2)), dma((2, rows // 2)), dma((3,)), dma((3,)),
        ],
        compiler_params=pltpu.CompilerParams(
            collective_id=0, has_side_effects=True, vmem_limit_bytes=40 << 20),
    )(*(
        pltpu.with_memory_space_constraint(x, pltpu.HBM)
        for x in (front, child, tile_group, row_map, row_map.reshape(1, -1))))


def final_kernel(front, left, right, own_p, groups, schur_hbm, panel, done, sem):
    r = lax.axis_index("row")
    c = lax.axis_index("col")
    rows, width = front.shape
    wide = done.shape[2]
    ii = lax.broadcasted_iota(jnp.int32, (rows, wide), 0)
    jj = lax.broadcasted_iota(jnp.int32, (rows, wide), 1)
    copies = []
    for g in range(width // wide):
        at = slice(g * wide, (g + 1) * wide)
        keep = jnp.logical_and(ii >= 16, lax.rem(jj + g * wide, MT) >= 16)
        coupled = jnp.where(groups[r] == groups[2 * c + (g * wide) // MT], 1.0, 0.0).astype(F32)
        total = front[:, at] * coupled + dot1(left[...], right[:, at], 1, 0)
        done[g] = jnp.where(keep, total, 0.0)
        copies.append(pltpu.make_async_copy(done.at[g], schur_hbm.at[:, pl.ds(g * wide, wide)], sem.at[g]))
        copies[-1].start()
    m = lax.broadcasted_iota(jnp.int32, (16, rows), 0) + c * 16
    a = lax.broadcasted_iota(jnp.int32, (16, rows), 1)
    p0 = own_p[0:16, :].astype(F32)
    p1 = own_p[16:32, :].astype(F32)
    p0 = jnp.where(jnp.logical_or(a >= 8, m <= r * 8 + a), p0, 0.0)
    p1 = jnp.where(jnp.logical_or(a >= 16, m <= r * 8 + a - 8), p1, 0.0)
    p1 = jnp.where(a >= 8, p1, 0.0)
    panel[0:16, :] = p0.astype(BF16)
    panel[16:32, :] = p1.astype(BF16)
    for copy in copies:
        copy.wait()


def final(front, left, right, own_p, tile_group):
    rows, width = front.shape
    step = 256
    vmem = pl.BlockSpec(memory_space=pltpu.VMEM)
    return pl.pallas_call(
        final_kernel,
        out_shape=(
            jax.ShapeDtypeStruct((rows, width), F32),
            jax.ShapeDtypeStruct((32, rows), BF16),
        ),
        in_specs=[vmem, vmem, vmem, vmem, pl.BlockSpec(memory_space=pltpu.SMEM)],
        out_specs=(pl.BlockSpec(memory_space=pltpu.HBM), vmem),
        scratch_shapes=[
            pltpu.VMEM((width // step, rows, step), F32),
            pltpu.SemaphoreType.DMA((width // step,)),
        ],
        compiler_params=pltpu.CompilerParams(vmem_limit_bytes=16 << 20),
    )(front, left, right, own_p, tile_group)


def local(front, tile_group, child, row_map):
    rows = lax.axis_size("row")
    cols = lax.axis_size("col")
    left, right, own_p = panels(front, child.T, tile_group, row_map, rows, cols)
    schur, panel = final(front, left, right, own_p, tile_group)
    return panel.T, schur


def solution(mesh):
    placed = (P("row", "col"), P(), P("row", "col"), P())
    return jax.shard_map(
        local,
        mesh=mesh,
        in_specs=placed,
        out_specs=(P("row", "col"), P("row", "col")),
        check_vma=False,
    )
```

```python
import functools

import jax
import jax.numpy as jnp
from jax import lax
from jax.experimental import pallas as pl
from jax.experimental.pallas import tpu as pltpu
from jax.sharding import PartitionSpec as P

PW = 256
NP = 2
TS = 128
MT = 512
NB = 64
F32 = jnp.float32
BF16 = jnp.bfloat16
MESH = pl.DeviceIdType.MESH


def loop(count, body):
    def step(i, carry):
        body(i)
        return carry

    lax.fori_loop(0, count, step, 0)


def split3(x):
    high = x.astype(BF16)
    rest = x - high.astype(F32)
    mid = rest.astype(BF16)
    return high, mid, (rest - mid.astype(F32)).astype(BF16)


def dot6(a, b, ca, cb):
    ah, am, al = split3(a)
    bh, bm, bl = split3(b)
    left = jnp.concatenate([ah, ah, am, ah, al, am], axis=ca)
    right = jnp.concatenate([bh, bm, bh, bl, bh, bm], axis=cb)
    return lax.dot_general(left, right, (((ca,), (cb,)), ((), ())), preferred_element_type=F32)


def dot1(a, b, ca, cb):
    return lax.dot_general(a, b, (((ca,), (cb,)), ((), ())), preferred_element_type=F32)


def block_inverse(block):
    ii = lax.broadcasted_iota(jnp.int32, (8, 128), 0)
    ll = lax.broadcasted_iota(jnp.int32, (8, 128), 1)
    groups = NB // 8
    m = []
    for g in range(groups):
        unit = jnp.where(ll == ii + (8 * g + NB), 1.0, 0.0).astype(F32)
        m.append(jnp.where(ll < NB, block[8 * g : 8 * g + 8, :], unit))
    for g in range(groups):
        low = 8 * g
        rows = [jnp.broadcast_to(m[g][i : i + 1, :], (8, 128)) for i in range(8)]
        cols = {}
        for h in range(g, groups):
            for k in range(8):
                cols[h, k] = jnp.broadcast_to(m[h][:, low + k : low + k + 1], (8, 128))
        for j in range(8):
            inv = lax.rsqrt(jnp.broadcast_to(cols[g, j][j : j + 1, :], (8, 128)))
            rows[j] = rows[j] * inv
            for h in range(g, groups):
                cols[h, j] = cols[h, j] * inv
            for k in range(j + 1, 8):
                factor = jnp.broadcast_to(cols[g, j][k : k + 1, :], (8, 128))
                for h in range(g, groups):
                    cols[h, k] = cols[h, k] - factor * cols[h, j]
                rows[k] = rows[k] - factor * rows[j]
        merged = rows[0]
        for i in range(1, 8):
            merged = jnp.where(ii == i, rows[i], merged)
        m[g] = merged
        for h in range(g + 1, groups):
            for j in range(8):
                m[h] = m[h] - cols[h, j] * rows[j]
    return jnp.concatenate(m, axis=0)[:, NB : 2 * NB]


def factor_step(work, b, beside, extra):
    lane = lax.broadcasted_iota(jnp.int32, (NB, PW), 1)
    beside(2 * b)
    here = pl.ds(pl.multiple_of(b * NB, NB), NB)
    band = work[here, :]
    lead = pltpu.roll(band[:, :PW], (PW - b * NB) % PW, axis=1)
    inverse = block_inverse(lead[:, :128])
    beside(2 * b + 1)
    extra(b)
    upper = dot6(inverse, band, 1, 0)
    below = jnp.where(lane >= (b + 1) * NB, upper[:, :PW], 0.0)
    work[...] -= dot6(below, upper, 0, 0)
    work[here, :] = upper


def split2(x, axis):
    high = x.astype(BF16)
    low = (x - high.astype(F32)).astype(BF16)
    return high, low


def left3(x):
    high, low = split2(x, 1)
    return jnp.concatenate([high, high, low], axis=1)


def right3(x, axis):
    high, low = split2(x, axis)
    return jnp.concatenate([high, low, high], axis=axis)


def front_kernel(
    front_hbm, child_hbm, groups_hbm, map_hbm, lanes_hbm,
    out_a, out_b, own_p,
    fcols, frows, child, groups, tile_map, map_lanes, in_s,
    zin, srow, zbuf, partner, placed, dpiece, vpiece,
    diag, vpiv, strip_r, strip_c, v_r, v_c, flags,
    work, wp, x0, x1, p01, turned_r, later,
    z_s, z_r, p_s, p_r, t_s, t_r,
    plane_s, plane_r, ring_s, ring_r, sib_s, sib_r, d_s, d_r,
):
    r = lax.axis_index("row")
    c = lax.axis_index("col")
    rows = lax.axis_size("row")
    cols = lax.axis_size("col")
    height, width = front_hbm.shape
    z = r // 2
    core = r % 2
    chips = rows // 2
    other = lax.rem(r + chips, rows)
    t_row = 2 * c + core
    t_col = z
    t_self = jnp.logical_and(t_row == r, t_col == c)

    barrier = pltpu.get_barrier_semaphore()

    loads = [
        pltpu.make_async_copy(src, dst, in_s.at[i])
        for i, (src, dst) in enumerate([
            (front_hbm.at[:, pl.ds(0, 128)], fcols.at[0]),
            (front_hbm.at[:, pl.ds(MT, 128)], fcols.at[1]),
            (child_hbm, child),
            (groups_hbm, groups),
            (map_hbm, tile_map),
            (front_hbm.at[pl.ds(0, 16), :], frows),
            (lanes_hbm, map_lanes),
        ])
    ]
    for load in loads:
        load.start()

    def hello(row, col):
        pl.semaphore_signal(barrier, inc=1, device_id=(row, col), device_id_type=MESH)

    loop(chips - 1, lambda i: hello(lax.rem(r + 2 * i + 2, rows), c))
    loop(cols - 1, lambda i: hello(r, lax.rem(c + i + 1, cols)))
    hello(2 * z + 1 - core, c)

    @pl.when(jnp.logical_not(t_self))
    def _():
        pl.semaphore_signal(barrier, inc=1, device_id=(t_row, t_col), device_id_type=MESH)

    def one_if(same):
        return jnp.where(same, 1.0, 0.0).astype(F32)

    for load in loads:
        load.wait()

    coupled = [one_if(groups[r] == groups[2 * c + q]) for q in range(2)]
    turned = []
    for q in range(2):
        t = jnp.transpose(fcols[q])[:16] * coupled[q]
        srow[0, 8 * q : 8 * q + 8, :] = t[:8]
        srow[1, 8 * q : 8 * q + 8, :] = t[8:]
        turned.append(t[:, :128])
    own_maps = [tile_map[4 * r + t] for t in range(4)]
    other_maps = [tile_map[4 * other + t] for t in range(4)]
    heads = []
    for target in (r, other):
        total = jnp.zeros((16, TS), F32)
        for t in range(4):
            total = total + child[:, t * TS : (t + 1) * TS].astype(F32) * one_if(own_maps[t] == 4 * target)
        heads.append(total)

    def second8(x):
        return pltpu.roll(x, 120, axis=1)

    tall = jnp.concatenate(
        [
            turned[0][:8], turned[1][:8], turned[0][8:], turned[1][8:],
            second8(turned[0])[8:], second8(turned[1])[8:], jnp.zeros((16, 128), F32),
            heads[0], heads[1], second8(heads[0]), second8(heads[1]),
        ],
        axis=0,
    )
    zin[...] = jnp.transpose(tall)[:8]

    pl.semaphore_wait(barrier, chips + cols - 1 + jnp.where(t_self, 0, 1))

    def z_copy(i):
        return pltpu.make_async_remote_copy(
            src_ref=zin, dst_ref=zbuf.at[core, z], send_sem=z_s.at[i], recv_sem=z_r.at[i],
            device_id=(lax.rem(r + 2 * i + 2, rows), c), device_id_type=MESH)

    def share_copy():
        return pltpu.make_async_remote_copy(
            src_ref=zbuf.at[core], dst_ref=zbuf.at[core],
            send_sem=z_s.at[chips - 1], recv_sem=z_r.at[chips - 1],
            device_id=(2 * z + 1 - core, c), device_id_type=MESH)

    def partner_copy():
        return pltpu.make_async_remote_copy(
            src_ref=child, dst_ref=partner, send_sem=p_s, recv_sem=p_r,
            device_id=(other, c), device_id_type=MESH)

    loop(chips - 1, lambda i: z_copy(i).start())
    partner_copy().start()
    zbuf[core, pl.ds(z, 1)] = zin[...][None]

    own16 = pl.ds(pl.multiple_of(c * 16, 16), 16)
    for q in range(2):
        at = slice(q * MT, (q + 1) * MT)
        strip_c[pl.ds(r, 1), :, at] = (frows[:, at] * coupled[q]).astype(BF16)[None]
    strip_r[:, own16, :] = srow[...]

    def slot(shift):
        return lax.rem(z + shift + chips, chips) * 2 + core

    def piece(a, row):
        return strip_c.at[row] if a == 0 else v_c.at[row]

    def ring_copy(a, way, distance):
        sign = 1 - 2 * way
        near = distance <= 2
        ref = piece(a, slot(0) if near else slot(-sign * (distance - 2)))
        return pltpu.make_async_remote_copy(
            src_ref=ref, dst_ref=ref,
            send_sem=ring_s.at[a, way, distance - 1], recv_sem=ring_r.at[a, way, distance - 1],
            device_id=(slot(sign * (distance if near else 2)), c), device_id_type=MESH)

    def sib_copy(a, row):
        ref = piece(a, row)
        return pltpu.make_async_remote_copy(
            src_ref=ref, dst_ref=ref, send_sem=sib_s.at[a, row // 2], recv_sem=sib_r.at[a, row // 2],
            device_id=(2 * z + 1 - core, c), device_id_type=MESH)

    hops = chips // 2

    def ring_pairs(stage):
        return [(way, d) for d in (2 * stage + 1, 2 * stage + 2) for way in range(2) if d < hops or way == 0]

    def ring_next(a, stage):
        if stage == 0:
            sib_copy(a, slot(0)).start()
        else:
            for way, d in ring_pairs(stage - 1):
                ring_copy(a, way, d).wait_recv()
        if stage < hops // 2:
            for way, d in ring_pairs(stage):
                ring_copy(a, way, d).start()
        if stage > 0:
            for way, d in ring_pairs(stage - 1):
                sib_copy(a, slot(-(1 - 2 * way) * d)).start()

    ring_next(0, 0)

    def plane_copy(a, src, dst, i):
        return pltpu.make_async_remote_copy(
            src_ref=src, dst_ref=dst, send_sem=plane_s.at[a, i], recv_sem=plane_r.at[a, i],
            device_id=(r, lax.rem(c + i + 1, cols)), device_id_type=MESH)

    def sr_copy(i):
        return plane_copy(0, srow, strip_r.at[:, own16, :], i)

    def d_copy(i):
        return plane_copy(1, dpiece.at[0], diag.at[0, own16, :], i)

    def d1_copy(i):
        return plane_copy(4, dpiece.at[1 + core], diag.at[1 + core, own16, :], i)

    def d1_share():
        return pltpu.make_async_remote_copy(
            src_ref=diag.at[1 + core], dst_ref=diag.at[1 + core], send_sem=d_s.at[0], recv_sem=d_r.at[0],
            device_id=(2 * z + 1 - core, c), device_id_type=MESH)

    def d_share():
        return pltpu.make_async_remote_copy(
            src_ref=diag.at[0], dst_ref=diag.at[0], send_sem=d_s.at[1], recv_sem=d_r.at[1],
            device_id=(2 * z + 1 - core, c), device_id_type=MESH)

    def vp_share():
        return pltpu.make_async_remote_copy(
            src_ref=vpiv, dst_ref=vpiv, send_sem=d_s.at[2], recv_sem=d_r.at[2],
            device_id=(2 * z + 1 - core, c), device_id_type=MESH)

    def vp_copy(i):
        return plane_copy(2, vpiece, vpiv.at[:, own16, :], i)

    def vr_copy(i):
        return plane_copy(3, placed, v_r.at[own16, :], i)

    partner_copy().wait_recv()
    for j in range(height // TS):
        total = jnp.zeros((16, TS), F32)
        for t in range(4):
            at = slice(t * TS, (t + 1) * TS)
            total = total + child[:, at].astype(F32) * one_if(own_maps[t] == 4 * r + j)
            total = total + partner[:, at].astype(F32) * one_if(other_maps[t] == 4 * r + j)
        placed[:, j * TS : (j + 1) * TS] = total.astype(BF16)
    v_r[own16, :] = placed[...]

    def t_copy():
        return pltpu.make_async_remote_copy(
            src_ref=placed, dst_ref=v_c.at[t_row], send_sem=t_s, recv_sem=t_r,
            device_id=(t_row, t_col), device_id_type=MESH)

    @pl.when(t_self)
    def _():
        v_c[pl.ds(r, 1)] = placed[...][None]

    @pl.when(jnp.logical_not(t_self))
    def _():
        t_copy().start()

    ring_next(0, 1)

    loop(chips - 1, lambda i: z_copy(i).wait_recv())
    share_copy().start()
    share_copy().wait_recv()
    flat = jnp.transpose(
        jnp.concatenate([zbuf[i % 2, i // 2] for i in range(rows)], axis=0))
    dpiece[0] = flat[0:16]
    dpiece[1] = flat[16:32]
    dpiece[2] = flat[32:48]
    half = rows * 4

    def swapped_halves(x):
        return jnp.concatenate([x[:, half:], x[:, :half]], axis=1)

    vpiece[0] = (flat[64:80] + swapped_halves(flat[80:96])).astype(BF16)
    vpiece[1] = (flat[96:112] + swapped_halves(flat[112:128])).astype(BF16)
    diag[1 + core, own16, :] = dpiece[1 + core]

    @pl.when(core == 0)
    def _():
        diag[0, own16, :] = dpiece[0]
        loop(cols - 1, lambda i: d_copy(i).start())

    @pl.when(core == 1)
    def _():
        vpiv[:, own16, :] = vpiece[...]
        loop(cols - 1, lambda i: vp_copy(i).start())

    loop(cols - 1, lambda i: d1_copy(i).start())

    loop(cols - 1, lambda i: vr_copy(i).start())
    loop(cols - 1, lambda i: sr_copy(i).start())

    @pl.when(jnp.logical_not(t_self))
    def _():
        t_copy().wait_recv()

    ring_next(1, 0)
    ring_next(0, 2)

    listed = jnp.transpose(jnp.broadcast_to(map_lanes[...].astype(F32), (128, 128)))
    count = map_lanes.shape[1]
    at_lane = lax.broadcasted_iota(jnp.int32, (128, 128), 1).astype(F32)
    child_id = lax.broadcasted_iota(jnp.int32, (128, 128), 0)
    hits = jnp.where(jnp.logical_and(listed == at_lane, child_id >= count // 2), 1.0, 0.0)
    second = jnp.broadcast_to(jnp.sum(hits, axis=0, keepdims=True), (8, 128)).astype(BF16)

    def spread(tile_of_lane, lanes):
        tile = lax.broadcasted_iota(jnp.int32, (128, lanes), 0)
        lane = lax.broadcasted_iota(jnp.int32, (128, lanes), 1)
        chosen = jnp.where(tile == tile_of_lane(lane), 1.0, 0.0).astype(BF16)
        return dot1(second, chosen, 1, 0).astype(BF16)

    flag_p = spread(lambda lane: 4 * lax.shift_right_logical(lane, 3), PW)[0:1]
    flags[0:8, :height] = spread(lambda lane: 4 * r + lax.shift_right_logical(lane, 7), height).astype(F32)
    flags[0:8, height:] = spread(lambda lane: 8 * c + lax.shift_right_logical(lane, 7), width).astype(F32)

    @pl.when(core == 0)
    def _():
        loop(cols - 1, lambda i: d_copy(i).wait_recv())
        d_share().start()
        vp_share().wait_recv()

    @pl.when(core == 1)
    def _():
        loop(cols - 1, lambda i: vp_copy(i).wait_recv())
        vp_share().start()
        d_share().wait_recv()

    for k in range(2):
        vp = vpiv[k]
        wp[k, PW:, :] = vp * flag_p
        wp[k, :PW, :] = vp - vp * flag_p
    i = lax.broadcasted_iota(jnp.int32, (PW, PW), 0)
    j = lax.broadcasted_iota(jnp.int32, (PW, PW), 1)
    eye = jnp.where(i == j, 1.0, 0.0).astype(F32)
    work[:, :PW] = diag[0] + dot1(wp[0], wp[0], 0, 0)
    work[:, PW:] = eye

    def beside(t):
        if t == 0:
            ring_next(0, 3)
            ring_next(1, 1)
        if t == 3:
            ring_next(1, 2)
        if t == 4:
            ring_next(0, 4)
        if t == 6:
            ring_next(1, 3)
        if t == 5:
            loop(cols - 1, lambda i: d1_copy(i).wait_recv())
            d1_share().start()

    for b in range(PW // NB):
        factor_step(work, b, beside, lambda b: None)
    x0[...] = left3(work[:, PW:])
    d1_share().wait_recv()
    low = diag[1] + dot1(wp[1], wp[0], 0, 0)
    p01[...] = dot1(right3(low, 1), x0[...], 1, 1).astype(BF16)

    work[:, :PW] = diag[2] + dot1(wp[1], wp[1], 0, 0) - dot1(p01[...], p01[...], 1, 1)
    work[:, PW:] = eye

    def first_part(strip0, strip1, v, flag):
        flag = flag.astype(BF16)
        bottom = v * flag
        w = jnp.concatenate([v - bottom, bottom], axis=0)
        s0 = strip0 + dot1(wp[0], w, 0, 0)
        first = dot1(x0[...], right3(s0, 0), 1, 0).astype(BF16)
        s1 = strip1 + dot1(wp[1], w, 0, 0) - dot1(p01[...], first, 1, 0)
        return w, first, right3(s1, 0)

    def col_tile(q, h):
        sub = slice(h * PW, (h + 1) * PW)
        at = slice(q * height + h * PW, q * height + (h + 1) * PW)
        v = jnp.concatenate([v_c[2 * i + q, :, sub] for i in range(chips)], axis=0)
        flag = flags[0:1, height + at.start : height + at.stop]
        strip = strip_c[:, :, at].astype(F32)
        w, first, rest = first_part(
            strip[:, :8].reshape(PW, PW), strip[:, 8:].reshape(PW, PW), v, flag)
        out_b[0 : 2 * PW, at] = w
        out_b[2 * PW : 3 * PW, at] = -first
        later[:, at] = rest

    tiles = [(q, h) for q in range(2) for h in range(height // PW)]

    def beside_second(t):
        if t == 1:
            ring_next(1, 4)
        if t == 4:
            for a in range(2):
                loop(chips, lambda i: sib_copy(a, 2 * i + core).wait_recv())

    def extra_second(b):
        if b == 2:
            col_tile(*tiles[0])
            col_tile(*tiles[1])
        if b == 3:
            col_tile(*tiles[2])
            col_tile(*tiles[3])

    for b in range(PW // NB):
        factor_step(work, b, beside_second, extra_second)
    x1[...] = left3(work[:, PW:])

    for q, h in tiles:
        at = slice(q * height + h * PW, q * height + (h + 1) * PW)
        out_b[3 * PW : 4 * PW, at] = -dot1(x1[...], later[:, at], 1, 0).astype(BF16)

    for copy in (sr_copy, vr_copy):
        loop(cols - 1, lambda i: copy(i).wait_recv())
    for h in range(height // PW):
        at = slice(h * PW, (h + 1) * PW)
        w, first, rest = first_part(
            strip_r[0, :, at], strip_r[1, :, at], v_r[:, at], flags[0:1, at])
        second = dot1(x1[...], rest, 1, 0).astype(BF16)
        turned_r[0:PW, at] = first
        turned_r[PW:, at] = second
        out_a[at, 0 : 2 * PW] = jnp.transpose(w)
        out_a[at, 2 * PW : 3 * PW] = jnp.transpose(first)
        out_a[at, 3 * PW : 4 * PW] = jnp.transpose(second)
    own_p[0:16, :] = turned_r[own16, :]
    own_p[16:32, :] = turned_r[pl.ds(pl.multiple_of(PW + c * 16, 16), 16), :]

    loop(chips - 1, lambda i: z_copy(i).wait_send())
    share_copy().wait_send()
    d1_share().wait_send()
    partner_copy().wait_send()

    @pl.when(jnp.logical_not(t_self))
    def _():
        t_copy().wait_send()

    @pl.when(core == 0)
    def _():
        d_share().wait_send()
        loop(cols - 1, lambda i: d_copy(i).wait_send())

    @pl.when(core == 1)
    def _():
        vp_share().wait_send()
        loop(cols - 1, lambda i: vp_copy(i).wait_send())

    for copy in (sr_copy, d1_copy, vr_copy):
        loop(cols - 1, lambda i: copy(i).wait_send())
    for a in range(2):
        loop(chips, lambda i: sib_copy(a, 2 * i + core).wait_send())
        for stage in range(hops // 2):
            for way, d in ring_pairs(stage):
                ring_copy(a, way, d).wait_send()


def panels(front, child, tile_group, row_map, rows, cols):
    vmem = pl.BlockSpec(memory_space=pltpu.VMEM)
    dma = pltpu.SemaphoreType.DMA
    shape = jax.ShapeDtypeStruct
    height, width = front.shape
    return pl.pallas_call(
        front_kernel,
        out_shape=(
            shape((height, 4 * PW), BF16), shape((4 * PW, width), BF16), shape((32, height), BF16)),
        in_specs=[pl.BlockSpec(memory_space=pltpu.HBM)] * 5,
        out_specs=(vmem, vmem, vmem),
        scratch_shapes=[
            pltpu.VMEM((2, height, 128), F32),
            pltpu.VMEM((16, width), F32),
            pltpu.VMEM((16, height), BF16),
            pltpu.SMEM(tile_group.shape, jnp.int32),
            pltpu.SMEM(row_map.shape, jnp.int32),
            pltpu.VMEM((1, row_map.shape[0]), jnp.int32),
            dma((7,)),
            pltpu.VMEM((8, 128), F32),
            pltpu.VMEM((2, 16, height), F32),
            pltpu.VMEM((2, rows // 2, 8, 128), F32),
            pltpu.VMEM((16, height), BF16),
            pltpu.VMEM((16, height), BF16),
            pltpu.VMEM((3, 16, PW), F32),
            pltpu.VMEM((2, 16, PW), BF16),
            pltpu.VMEM((3, PW, PW), F32),
            pltpu.VMEM((2, PW, PW), BF16),
            pltpu.VMEM((2, PW, height), F32),
            pltpu.VMEM((rows, 16, width), BF16),
            pltpu.VMEM((PW, height), BF16),
            pltpu.VMEM((rows, 16, height), BF16),
            pltpu.VMEM((8, height + width), F32),
            pltpu.VMEM((PW, 2 * PW), F32),
            pltpu.VMEM((2, 2 * PW, PW), BF16),
            pltpu.VMEM((PW, 3 * PW), BF16),
            pltpu.VMEM((PW, 3 * PW), BF16),
            pltpu.VMEM((PW, PW), BF16),
            pltpu.VMEM((2 * PW, height), BF16),
            pltpu.VMEM((3 * PW, width), BF16),
            dma((rows // 2,)), dma((rows // 2,)), dma, dma, dma, dma,
            dma((5, cols - 1)), dma((5, cols - 1)),
            dma((2, 2, rows // 4)), dma((2, 2, rows // 4)),
            dma((2, rows // 2)), dma((2, rows // 2)), dma((3,)), dma((3,)),
        ],
        compiler_params=pltpu.CompilerParams(
            collective_id=0, has_side_effects=True, vmem_limit_bytes=40 << 20),
    )(*(
        pltpu.with_memory_space_constraint(x, pltpu.HBM)
        for x in (front, child, tile_group, row_map, row_map.reshape(1, -1))))


def final_kernel(front, left, right, own_p, groups, schur_hbm, panel, done, sem):
    r = lax.axis_index("row")
    c = lax.axis_index("col")
    rows, width = front.shape
    wide = done.shape[2]
    ii = lax.broadcasted_iota(jnp.int32, (rows, wide), 0)
    jj = lax.broadcasted_iota(jnp.int32, (rows, wide), 1)
    copies = []
    for g in range(width // wide):
        at = slice(g * wide, (g + 1) * wide)
        keep = jnp.logical_and(ii >= 16, lax.rem(jj + g * wide, MT) >= 16)
        coupled = jnp.where(groups[r] == groups[2 * c + (g * wide) // MT], 1.0, 0.0).astype(F32)
        total = front[:, at] * coupled + dot1(left[...], right[:, at], 1, 0)
        done[g] = jnp.where(keep, total, 0.0)
        copies.append(pltpu.make_async_copy(done.at[g], schur_hbm.at[:, pl.ds(g * wide, wide)], sem.at[g]))
        copies[-1].start()
    m = lax.broadcasted_iota(jnp.int32, (16, rows), 0) + c * 16
    a = lax.broadcasted_iota(jnp.int32, (16, rows), 1)
    p0 = own_p[0:16, :].astype(F32)
    p1 = own_p[16:32, :].astype(F32)
    p0 = jnp.where(jnp.logical_or(a >= 8, m <= r * 8 + a), p0, 0.0)
    p1 = jnp.where(jnp.logical_or(a >= 16, m <= r * 8 + a - 8), p1, 0.0)
    p1 = jnp.where(a >= 8, p1, 0.0)
    panel[0:16, :] = p0.astype(BF16)
    panel[16:32, :] = p1.astype(BF16)
    for copy in copies:
        copy.wait()


def final(front, left, right, own_p, tile_group):
    rows, width = front.shape
    step = 256
    vmem = pl.BlockSpec(memory_space=pltpu.VMEM)
    return pl.pallas_call(
        final_kernel,
        out_shape=(
            jax.ShapeDtypeStruct((rows, width), F32),
            jax.ShapeDtypeStruct((32, rows), BF16),
        ),
        in_specs=[vmem, vmem, vmem, vmem, pl.BlockSpec(memory_space=pltpu.SMEM)],
        out_specs=(pl.BlockSpec(memory_space=pltpu.HBM), vmem),
        scratch_shapes=[
            pltpu.VMEM((width // step, rows, step), F32),
            pltpu.SemaphoreType.DMA((width // step,)),
        ],
        compiler_params=pltpu.CompilerParams(vmem_limit_bytes=16 << 20),
    )(front, left, right, own_p, tile_group)


def local(front, tile_group, child, row_map):
    rows = lax.axis_size("row")
    cols = lax.axis_size("col")
    left, right, own_p = panels(front, child.T, tile_group, row_map, rows, cols)
    schur, panel = final(front, left, right, own_p, tile_group)
    return panel.T, schur


def solution(mesh):
    placed = (P("row", "col"), P(), P("row", "col"), P())
    return jax.shard_map(
        local,
        mesh=mesh,
        in_specs=placed,
        out_specs=(P("row", "col"), P("row", "col")),
        check_vma=False,
    )
```
